256 devices in a mesh: fsdp: 32 (over z, y), tp: 8 (over x, core).
Axes of the slice: x: 4, y: 4, z: 8, core: 2. Of those that a mesh axis runs over, the one named last changes fastest.
Arguments:
- tokens: bfloat16 [8192, 4096], P('fsdp', 'tp'), may hold values from -6 to 6
- cotangent: bfloat16 [8192, 4096], P('fsdp', 'tp'), may hold values from -6 to 6
- up_weight: bfloat16 [4096, 14336], P('fsdp', 'tp'), may hold values from -0.1875 to 0.1875
- down_weight: bfloat16 [4096, 14336], P('fsdp', 'tp'), may hold values from -0.09375 to 0.09375
- up_list: int32 [8, 128, 2], P('tp'), may hold values from 0 to 31, as said below
- up_count: int32 [8], P('tp'), may hold values from 35 to 128, as said below
- down_list: int32 [8, 128, 2], P('tp'), may hold values from 0 to 31, as said below
- down_count: int32 [8], P('tp'), may hold values from 35 to 128, as said below
Outputs:
- mixed: bfloat16 [8192, 4096], P('fsdp', 'tp')
- grad_tokens: bfloat16 [8192, 4096], P('fsdp', 'tp')
- grad_up: float32 [4096, 14336], P('fsdp', 'tp')
- grad_down: float32 [4096, 14336], P('fsdp', 'tp')
The draws below stay inside these ranges and needn't reach their ends.
Inputs may be any that keep to these rules, and one draw needn't show every extreme that they name: `up_list`: in each slice's list the first count entries are distinct pairs (row block below 32, column block below 14), in no particular order; every row block has at least one and at most 4 of them; in every slice the one row block held by some index of fsdp have exactly 4, and in some slice every row block has exactly 4. Entries from the count on are arbitrary pairs in range and carry no meaning. `up_count`: the number of valid entries of each slice's up list. `down_list`: as for up_list. `down_count`: the number of valid entries of each slice's down list.
All inputs are finite; a program needn't handle non-finite values.
Results may differ from the reference program's by a relative error of at most 0.015.
Values may be sent and summed in bfloat16 or wider, within the bound.
No kernel may reach another device: no remote copies, remote signals or barrier semaphores. Data moves between devices by JAX's collectives and lax.ppermute only.
A program may use at most 256 MiB of HBM per device.

```python
import jax
import jax.numpy as jnp
from jax import lax

D = 4096
FF = 14336
BLK = 128
GROUP_TOK = 256
TOKENS = 8192
DB = 32
FBT = 14
RB = 1
CAPR = 4
LIST = 128
N_FSDP = 32
N_TP = 8


def list_draw(key, salt):
    folded = jax.random.fold_in(key, salt)
    keys = jax.random.split(folded, 7)
    counts = jax.random.randint(keys[0], (N_TP, DB), 1, CAPR + 1)
    full_owner = jax.random.randint(keys[1], (N_TP, 1), 0, N_FSDP)
    row_ids = jnp.arange(DB, dtype=jnp.int32)[None, :]
    counts = jnp.where(row_ids // RB == full_owner, CAPR, counts)
    full_slice = jax.random.randint(keys[6], (), 0, N_TP)
    slice_ids = jnp.arange(N_TP, dtype=jnp.int32)[:, None]
    counts = jnp.where(slice_ids == full_slice, CAPR, counts)
    perm_keys = jax.random.split(keys[2], N_TP * DB)
    perms = jax.vmap(lambda single: jax.random.permutation(single, FBT))(perm_keys)
    chosen = perms.reshape(N_TP, DB, FBT)[:, :, :CAPR].astype(jnp.int32)
    valid = jnp.arange(CAPR, dtype=jnp.int32)[None, None, :] < counts[:, :, None]
    rows = jnp.broadcast_to(jnp.arange(DB, dtype=jnp.int32)[None, :, None], (N_TP, DB, CAPR))
    rows = rows.reshape(N_TP, LIST)
    cols = chosen.reshape(N_TP, LIST)
    valid = valid.reshape(N_TP, LIST)
    scores = jax.random.randint(keys[3], (N_TP, LIST), 0, 1 << 20)
    scores = jnp.where(valid, scores, 1 << 20) * LIST + jnp.arange(LIST, dtype=jnp.int32)[None, :]
    order = jnp.argsort(scores, axis=1)
    rows = jnp.take_along_axis(rows, order, axis=1)
    cols = jnp.take_along_axis(cols, order, axis=1)
    valid = jnp.take_along_axis(valid, order, axis=1)
    filler_rows = jax.random.randint(keys[4], (N_TP, LIST), 0, DB)
    filler_cols = jax.random.randint(keys[5], (N_TP, LIST), 0, FBT)
    rows = jnp.where(valid, rows, filler_rows)
    cols = jnp.where(valid, cols, filler_cols)
    entries = jnp.stack([rows, cols], axis=-1).astype(jnp.int32)
    number = jnp.sum(valid.astype(jnp.int32), axis=1).astype(jnp.int32)
    return (entries, number)


def draw_up_list(key, part):
    return list_draw(key, 11)[0]


def draw_up_count(key, part):
    return list_draw(key, 11)[1]


def draw_down_list(key, part):
    return list_draw(key, 23)[0]


def draw_down_count(key, part):
    return list_draw(key, 23)[1]


def with_spikes(values, own_key, source, target, blocks, factor):
    owner, partner = [(jnp.arange(values.shape[position]) // (values.shape[position] // blocks)).reshape([-1 if axis == position else 1 for axis in range(values.ndim)]) for position in (source, target)]
    chosen = jax.random.permutation(own_key, blocks)[partner]
    strong = (owner == chosen) | (owner == (partner + blocks // 2) % blocks)
    return jnp.where(strong, factor * values, values)


def steps_of(stream_key, extent, shards, smallest, top_value):
    factor_of = 1.0
    for axis_at, blocks in shards:
        heights = jax.random.uniform(jax.random.fold_in(jax.random.fold_in(stream_key, 6), axis_at), (blocks,), jnp.float32, smallest / len(shards), top_value / len(shards))
        factor_of = factor_of * jnp.repeat(jnp.exp(heights), extent[axis_at] // blocks).reshape((-1,) + (1,) * (len(extent) - 1 - axis_at))
    return factor_of


def gaussian(own_key, dims, scale, limit, cuts=(), kind=jnp.bfloat16):
    values = scale * jax.random.normal(own_key, dims, jnp.float32)
    if cuts:
        values = values * steps_of(own_key, dims, cuts, -0.22, 0.18)
    return jnp.clip(values, -limit, limit).astype(kind)


def gaussian_with(stream_key, dims, scale, most, pieces, heavy, held_as=jnp.bfloat16):
    array = scale * jax.random.normal(stream_key, dims, jnp.float32)
    if pieces:
        array = array * steps_of(stream_key, dims, pieces, -0.22, 0.18)
    return jnp.clip(with_spikes(array, jax.random.fold_in(stream_key, 3), *heavy), -most, most).astype(held_as)


def setup_inputs(seed: int = 0) -> dict:
    key_of = jax.random.split(jax.random.key(seed), 9)
    tokens = gaussian_with(key_of[0], (TOKENS, D), 1.0, 6.0, ((0, 32), (1, 8)), (0, 1, 32, 2.75))
    cotangent = gaussian_with(key_of[1], (TOKENS, D), 1.0, 6.0, ((0, 32), (1, 8)), (0, 1, 32, 2.75))
    up_weight = gaussian(key_of[2], (D, FF), (D // 4) ** -0.5, 0.1875, ((0, 32), (1, 8)))
    down_weight = gaussian(key_of[3], (D, FF), (FF // 4) ** -0.5, 0.09375, ((0, 32), (1, 8)))
    up_list = draw_up_list(jax.random.fold_in(key_of[8], 71), 0)
    up_count = draw_up_count(jax.random.fold_in(key_of[8], 71), 0)
    down_list = draw_down_list(jax.random.fold_in(key_of[8], 71), 0)
    down_count = draw_down_count(jax.random.fold_in(key_of[8], 71), 0)
    return {"tokens": tokens, "cotangent": cotangent, "up_weight": up_weight, "down_weight": down_weight, "up_list": up_list, "up_count": up_count, "down_list": down_list, "down_count": down_count}


SQRT_TWO_PI = 0.7978845608028654
CUBIC = 0.044715


def gelu_tanh(values):
    inner = SQRT_TWO_PI * (values + CUBIC * values * values * values)
    return 0.5 * values * (1.0 + jnp.tanh(inner))


def gelu_slope(values):
    tangent = jnp.tanh(SQRT_TWO_PI * (values + CUBIC * values * values * values))
    return 0.5 * (1.0 + tangent) + 0.5 * values * (1.0 - tangent * tangent) * SQRT_TWO_PI * (1.0 + 3.0 * CUBIC * values * values)


def list_tables(entries, number):
    rows = entries[:, :, 0].astype(jnp.int32)
    offsets = (jnp.arange(N_TP, dtype=jnp.int32) * FBT)[:, None]
    cols = entries[:, :, 1].astype(jnp.int32) + offsets
    valid = jnp.arange(LIST, dtype=jnp.int32)[None, :] < number[:, None]
    return rows, cols, valid


def blocks_of(weight, rows, cols, valid):
    tiles = weight.reshape(DB, BLK, FF // BLK, BLK)
    picked = tiles[rows, :, cols, :]
    return jnp.where(valid[:, :, None, None], picked, jnp.zeros((), weight.dtype))


def rounded_sum(parts):
    narrow = lax.optimization_barrier(parts.astype(jnp.bfloat16))
    return jnp.sum(narrow.astype(jnp.float32), axis=1)


def reference(tokens, cotangent, up_weight, down_weight, up_list, up_count, down_list, down_count):
    up_rows, up_cols, up_valid = list_tables(up_list, up_count)
    down_rows, down_cols, down_valid = list_tables(down_list, down_count)
    up_tiles = blocks_of(up_weight, up_rows, up_cols, up_valid).astype(jnp.float32)
    down_tiles = blocks_of(down_weight, down_rows, down_cols, down_valid).astype(jnp.float32)
    slice_ids = jnp.arange(N_TP, dtype=jnp.int32)[:, None]
    token_groups = tokens.reshape(N_FSDP, GROUP_TOK, D)
    grad_groups = cotangent.reshape(N_FSDP, GROUP_TOK, D)

    def group_step(carry, group):
        x_group, dy_group = group
        x_tiles = x_group.reshape(GROUP_TOK, DB, BLK)
        dy_tiles = dy_group.reshape(GROUP_TOK, DB, BLK)
        x_taken = x_tiles[:, up_rows, :].astype(jnp.float32)
        partial_up = jnp.einsum('rtlk,tlkn->rtln', x_taken, up_tiles)
        hidden = jnp.zeros((GROUP_TOK, FF // BLK, BLK), jnp.float32).at[:, up_cols, :].add(partial_up)
        active = gelu_tanh(hidden).astype(jnp.bfloat16)
        active_taken = active[:, down_cols, :].astype(jnp.float32)
        partial_down = jnp.einsum('rtln,tlkn->rtlk', active_taken, down_tiles)
        layer_parts = jnp.zeros((GROUP_TOK, N_TP, DB, BLK), jnp.float32).at[:, slice_ids, down_rows, :].add(partial_down)
        mixed = rounded_sum(layer_parts).reshape(GROUP_TOK, D).astype(jnp.bfloat16)
        dy_taken = dy_tiles[:, down_rows, :].astype(jnp.float32)
        back_down = jnp.einsum('rtlk,tlkn->rtln', dy_taken, down_tiles)
        grad_active = jnp.zeros((GROUP_TOK, FF // BLK, BLK), jnp.float32).at[:, down_cols, :].add(back_down)
        grad_hidden = (grad_active * gelu_slope(hidden)).astype(jnp.bfloat16)
        hidden_taken = grad_hidden[:, up_cols, :].astype(jnp.float32)
        back_up = jnp.einsum('rtln,tlkn->rtlk', hidden_taken, up_tiles)
        input_parts = jnp.zeros((GROUP_TOK, N_TP, DB, BLK), jnp.float32).at[:, slice_ids, up_rows, :].add(back_up)
        grad_tokens = rounded_sum(input_parts).reshape(GROUP_TOK, D).astype(jnp.bfloat16)
        up_term = jnp.einsum('rtlk,rtln->tlkn', x_taken, hidden_taken)
        down_term = jnp.einsum('rtlk,rtln->tlkn', dy_taken, active_taken)
        up_term = lax.optimization_barrier(up_term.astype(jnp.bfloat16)).astype(jnp.float32)
        down_term = lax.optimization_barrier(down_term.astype(jnp.bfloat16)).astype(jnp.float32)
        return (carry[0] + up_term, carry[1] + down_term), (mixed, grad_tokens)

    start_sums = (jnp.zeros((N_TP, LIST, BLK, BLK), jnp.float32), jnp.zeros((N_TP, LIST, BLK, BLK), jnp.float32))
    sums, outputs = lax.scan(group_step, start_sums, (token_groups, grad_groups))
    mixed = outputs[0].reshape(TOKENS, D)
    grad_tokens = outputs[1].reshape(TOKENS, D)
    up_sum = jnp.where(up_valid[:, :, None, None], sums[0], jnp.zeros((), jnp.float32))
    down_sum = jnp.where(down_valid[:, :, None, None], sums[1], jnp.zeros((), jnp.float32))
    grad_up = jnp.zeros((DB, BLK, FF // BLK, BLK), jnp.float32).at[up_rows, :, up_cols, :].add(up_sum).reshape(D, FF)
    grad_down = jnp.zeros((DB, BLK, FF // BLK, BLK), jnp.float32).at[down_rows, :, down_cols, :].add(down_sum).reshape(D, FF)
    return (mixed, grad_tokens, grad_up, grad_down)
```

```python
import functools

import jax
import jax.numpy as jnp
from jax import lax
from jax.experimental import pallas as pl
from jax.experimental.pallas import tpu as pltpu
from jax.sharding import PartitionSpec as P

BLK = 128
CAP = 4
NZ, NY, NX = 8, 4, 4
FBT = 14
TOK = 256
ROWS = NZ * NY
FEAT = NY * BLK

SQRT_TWO_PI = 0.7978845608028654
CUBIC = 0.044715

ZD = (0, -1, 1, -2, 2, -3, 3, 4)
YD = (0, -1, 1, 2)

BF16 = jnp.bfloat16
F32 = jnp.float32


def shift_fsdp(value, dz, dy):
    pairs = []
    for z in range(NZ):
        for y in range(NY):
            pairs.append((z * NY + y, ((z + dz) % NZ) * NY + (y + dy) % NY))
    return lax.ppermute(value, "fsdp", pairs)


def shift_x(value, dx):
    return lax.ppermute(value, "tp", [(i, (i + 2 * dx) % 8) for i in range(8)])


def partner(value):
    return lax.ppermute(value, "tp", [(i, i ^ 1) for i in range(8)])


def abs_z(meta, dz):
    return (meta[0] + dz) & (NZ - 1)


def abs_y(meta, dy):
    return (meta[1] + dy) & (NY - 1)


def x_place(meta, zz):
    return ((zz & 1) ^ meta[3]) * NX + ((meta[2] - (zz >> 1)) & (NX - 1))


def lanes(index):
    return pl.ds(pl.multiple_of(index * BLK, BLK), BLK)


def full(shape):
    return pl.BlockSpec(shape, lambda i, meta, cols: (0,) * len(shape))


def features_of_z(dz):
    return pl.BlockSpec(
        (1, TOK, FEAT), lambda i, meta, cols: (x_place(meta, abs_z(meta, dz)), 0, 0)
    )


def features_of_y(dy):
    return pl.BlockSpec((NZ, TOK, BLK), lambda i, meta, cols: (0, 0, abs_y(meta, dy)))


def read_features(kind, ref, meta, dz, dy):
    if kind == "z":
        return ref[0, :, lanes(abs_y(meta, dy))]
    return ref[x_place(meta, abs_z(meta, dz))]


def slot_cols(meta, cols, dz, dy):
    base = (abs_z(meta, dz) * NY + abs_y(meta, dy)) * CAP
    return [jnp.maximum(cols[base + j], 0) for j in range(CAP)]


def call(kernel, meta, cols, operands, specs, outs, out_specs, aliases=None):
    return pl.pallas_call(
        kernel,
        out_shape=outs,
        grid_spec=pltpu.PrefetchScalarGridSpec(
            num_scalar_prefetch=2,
            grid=(1,),
            in_specs=specs,
            out_specs=out_specs,
        ),
        input_output_aliases=aliases or {},
    )(meta, cols, *operands)


def pick(meta, both_cols, up_weight, down_weight):
    def kernel(meta, cols, up_ref, down_ref, up_out, down_out):
        base = (meta[0] * NY + meta[1]) * CAP
        for part, (source, target) in enumerate(((up_ref, up_out), (down_ref, down_out))):
            for j in range(CAP):
                col = cols[part, base + j]

                @pl.when(col >= 0)
                def _():
                    target[j] = source[:, lanes(jnp.maximum(col, 0))]

                @pl.when(col < 0)
                def _():
                    target[j] = jnp.zeros((BLK, BLK), BF16)

    shape = jax.ShapeDtypeStruct((CAP, BLK, BLK), BF16)
    spec = full((CAP, BLK, BLK))
    return call(
        kernel,
        meta,
        both_cols,
        (up_weight, down_weight),
        [full(up_weight.shape), full(down_weight.shape)],
        (shape, shape),
        (spec, spec),
    )


def accumulate(meta, cols, kind, features, feature_keys, chunks, rows, acc):
    count = len(feature_keys)

    def kernel(meta, cols, *refs):
        x_refs, chunk_refs = refs[:count], refs[count : count + len(chunks)]
        out = refs[-1]
        if acc is None:
            out[...] = jnp.zeros_like(out)
        else:
            out[...] = refs[-2][...]
        for xi, ci, base, dz, dy in rows:
            left = read_features(kind, x_refs[xi], meta, dz, dy)
            right = jnp.concatenate([chunk_refs[ci][base + j] for j in range(CAP)], axis=1)
            product = jnp.dot(left, right, preferred_element_type=F32)
            for j, col in enumerate(slot_cols(meta, cols, dz, dy)):
                out[col] += product[:, j * BLK : (j + 1) * BLK]

    make = features_of_z if kind == "z" else features_of_y
    specs = [make(key) for key in feature_keys] + [full(c.shape) for c in chunks]
    operands = [features] * count + list(chunks)
    aliases = {}
    if acc is not None:
        specs.append(full(acc.shape))
        operands.append(acc)
        aliases = {1 + len(operands): 0}
    return call(
        kernel,
        meta,
        cols,
        operands,
        specs,
        jax.ShapeDtypeStruct((FBT, TOK, BLK), F32),
        full((FBT, TOK, BLK)),
        aliases,
    )


def activate(meta, cols, hidden, grad_active):
    def kernel(meta, cols, h_ref, g_ref, act, act_t, grad, grad_t):
        v = h_ref[0]
        tangent = jnp.tanh(SQRT_TWO_PI * (v + CUBIC * v * v * v))
        a = (0.5 * v * (1.0 + tangent)).astype(BF16)
        slope = 0.5 * (1.0 + tangent) + 0.5 * v * (1.0 - tangent * tangent) * SQRT_TWO_PI * (
            1.0 + 3.0 * CUBIC * v * v
        )
        g = (g_ref[0] * slope).astype(BF16)
        act[0] = a
        act_t[0] = a.T
        grad[0] = g
        grad_t[0] = g.T

    spec = pl.BlockSpec((1, TOK, BLK), lambda i, meta, cols: (i, 0, 0))
    spec_t = pl.BlockSpec((1, BLK, TOK), lambda i, meta, cols: (i, 0, 0))
    shape = jax.ShapeDtypeStruct((FBT, TOK, BLK), BF16)
    shape_t = jax.ShapeDtypeStruct((FBT, BLK, TOK), BF16)
    return pl.pallas_call(
        kernel,
        out_shape=(shape, shape_t, shape, shape_t),
        grid_spec=pltpu.PrefetchScalarGridSpec(
            num_scalar_prefetch=2,
            grid=(FBT,),
            in_specs=[spec, spec],
            out_specs=(spec, spec_t, spec, spec_t),
        ),
    )(meta, cols, hidden, grad_active)


def terms(meta, cols, kind, units_t, features, feature_keys, received, sizes, rows):
    count = len(feature_keys)

    def kernel(meta, cols, units, *refs):
        x_refs = refs[:count]
        got = refs[count : count + len(received)]
        outs = refs[count + len(received) :]
        for xi, dz, dy, oi, base, adds in rows:
            right = read_features(kind, x_refs[xi], meta, dz, dy)
            left = jnp.concatenate([units[c] for c in slot_cols(meta, cols, dz, dy)], axis=0)
            product = jnp.dot(left, right, preferred_element_type=F32)
            total = product.reshape(CAP, BLK, BLK)
            for gi, start in adds:
                total = total + got[gi][start : start + CAP].astype(F32)
            outs[oi][base : base + CAP] = total.astype(BF16)

    make = features_of_z if kind == "z" else features_of_y
    specs = [full(units_t.shape)] + [make(key) for key in feature_keys]
    specs += [full(r.shape) for r in received]
    return call(
        kernel,
        meta,
        cols,
        [units_t] + [features] * count + list(received),
        specs,
        tuple(jax.ShapeDtypeStruct((size, BLK, BLK), BF16) for size in sizes),
        tuple(full((size, BLK, BLK)) for size in sizes),
    )


def project(meta, cols, units, chunks, rows):
    def kernel(meta, cols, units_ref, *refs):
        chunk_refs, (same, other) = refs[: len(chunks)], refs[len(chunks) :]
        for ci, base, dz, dy in rows:
            left = jnp.concatenate(
                [units_ref[c] for c in slot_cols(meta, cols, dz, dy)], axis=1
            )
            right = jnp.concatenate([chunk_refs[ci][base + j] for j in range(CAP)], axis=1)
            product = lax.dot_general(
                left, right, (((1,), (1,)), ((), ())), preferred_element_type=F32
            ).astype(BF16)
            zz = abs_z(meta, dz)
            place = ((zz >> 1) - meta[2]) & (NX - 1)
            where = lanes(abs_y(meta, dy))
            mine = (zz & 1) == meta[3]

            @pl.when(mine)
            def _():
                same[place, :, where] = product

            @pl.when(jnp.logical_not(mine))
            def _():
                other[place, :, where] = product

    shape = jax.ShapeDtypeStruct((NX, TOK, FEAT), BF16)
    spec = full((NX, TOK, FEAT))
    return call(
        kernel,
        meta,
        cols,
        [units] + list(chunks),
        [full(units.shape)] + [full(c.shape) for c in chunks],
        (shape, shape),
        (spec, spec),
    )


def place_grads(meta, cols, pieces):
    def kernel(meta, cols, *refs):
        out = refs[-1]
        out[...] = jnp.zeros_like(out)
        base = (meta[0] * NY + meta[1]) * CAP
        for j in range(CAP):
            total = refs[0][j].astype(F32)
            for ref in refs[1:-1]:
                total = total + ref[j].astype(F32)
            col = cols[base + j]

            @pl.when(col >= 0)
            def _():
                out[:, lanes(jnp.maximum(col, 0))] = total.T

    return call(
        kernel,
        meta,
        cols,
        pieces,
        [full(p.shape) for p in pieces],
        jax.ShapeDtypeStruct((BLK, FBT * BLK), F32),
        full((BLK, FBT * BLK)),
    )


def column_tables(lists, counts):
    rows, cols = lists[:, :, 0], lists[:, :, 1]
    index = jnp.arange(lists.shape[1], dtype=jnp.int32)
    valid = index[None, :] < counts[:, None]
    rows = jnp.where(valid, rows, -1)
    same = (rows[:, :, None] == rows[:, None, :]) & (index[None, None, :] < index[None, :, None])
    rank = jnp.sum(same.astype(jnp.int32), axis=2)
    slot = jnp.where(valid, rows * CAP + rank, -1)
    chosen = slot[:, None, :] == index[None, :, None]
    return jnp.sum(jnp.where(chosen, cols[:, None, :] + 1, 0), axis=2) - 1


def gather_features(shard):
    own = jnp.stack([shard] + [shift_x(shard, k) for k in (1, 2, 3)])
    return jnp.concatenate([own, partner(own)], axis=0)


def reduce_features(same, other):
    got = partner(other)
    pair = [(same[k].astype(F32) + got[k].astype(F32)).astype(BF16) for k in range(NX)]
    total = pair[0].astype(F32)
    for k in (1, 2, 3):
        total = total + shift_x(pair[k], k).astype(F32)
    return total.astype(BF16)


def body(tokens, cotangent, up_weight, down_weight, up_list, up_count, down_list, down_count):
    group, slice_id = lax.axis_index("fsdp"), lax.axis_index("tp")
    meta = jnp.stack([group // NY, group % NY, slice_id // 2, slice_id % 2]).astype(jnp.int32)
    tables = column_tables(
        jnp.concatenate([up_list, down_list]), jnp.concatenate([up_count, down_count])
    )
    up_cols, down_cols = tables[0], tables[1]
    up_own, down_own = pick(meta, tables, up_weight, down_weight)

    u = jnp.concatenate([up_own] + [shift_fsdp(up_own, 0, -d) for d in YD[1:]])
    da1, db1 = shift_fsdp(down_own, 1, 0), shift_fsdp(down_own, -1, 0)
    x_all = gather_features(tokens)
    ua1, ub1 = shift_fsdp(u, 1, 0), shift_fsdp(u, -1, 0)
    da2, db2 = shift_fsdp(da1, 1, 0), shift_fsdp(db1, -1, 0)
    da3, db3 = shift_fsdp(da2, 1, 0), shift_fsdp(db2, -1, 0)
    da4 = shift_fsdp(da3, 1, 0)
    dn = jnp.concatenate([down_own, da1, db1, da2, db2, da3, db3, da4])
    dc1, dd1 = shift_fsdp(dn, 0, 1), shift_fsdp(dn, 0, -1)
    ua2, ub2 = shift_fsdp(ua1, 1, 0), shift_fsdp(ub1, -1, 0)
    dy_all = gather_features(cotangent)
    ua3, ub3 = shift_fsdp(ua2, 1, 0), shift_fsdp(ub2, -1, 0)
    dc2, dd2 = shift_fsdp(dc1[:16], 0, 1), shift_fsdp(dd1[16:], 0, -1)
    ua4, ub4 = shift_fsdp(ua3[:8], 1, 0), shift_fsdp(ub3[8:], -1, 0)

    def z_rows(operand, dz):
        return [(operand, operand, i * CAP, dz, YD[i]) for i in range(NY)]

    def y_rows(operand, dy):
        return [(operand, operand, i * CAP, ZD[i], dy) for i in range(NZ)]

    hidden = accumulate(
        meta, up_cols, "z", x_all, (0, -1, 1), (u, ua1, ub1),
        z_rows(0, 0) + z_rows(1, -1) + z_rows(2, 1), None,
    )
    hidden = accumulate(
        meta, up_cols, "z", x_all, (-2, 2), (ua2, ub2), z_rows(0, -2) + z_rows(1, 2), hidden
    )
    hidden = accumulate(
        meta, up_cols, "z", x_all, (-3, 3), (ua3, ub3), z_rows(0, -3) + z_rows(1, 3), hidden
    )
    hidden = accumulate(
        meta, up_cols, "z", x_all, (4,), (ua4, ub4),
        [(0, i // 2, (i % 2) * CAP, 4, YD[i]) for i in range(NY)], hidden,
    )
    grad_active = accumulate(
        meta, down_cols, "y", dy_all, (0,), (dn,), y_rows(0, 0), None
    )
    grad_active = accumulate(
        meta, down_cols, "y", dy_all, (-1, 1), (dc1, dd1),
        y_rows(0, -1) + y_rows(1, 1), grad_active,
    )
    grad_active = accumulate(
        meta, down_cols, "y", dy_all, (2,), (dc2, dd2),
        [(0, i // 4, (i % 4) * CAP, ZD[i], 2) for i in range(NZ)], grad_active,
    )
    active, active_t, grad_hidden, grad_hidden_t = activate(meta, up_cols, hidden, grad_active)

    up_terms = functools.partial(terms, meta, up_cols, "z", grad_hidden_t, x_all)
    down_terms = functools.partial(terms, meta, down_cols, "y", active_t, dy_all)

    def z_terms(operand, dz, out, adds):
        return [
            (operand, dz, YD[i], out, i * CAP, [(g, s + i * CAP) for g, s, lo, hi in adds if lo <= i < hi])
            for i in range(NY)
        ]

    def y_terms(operand, dy, out, adds):
        return [
            (operand, ZD[i], dy, out, i * CAP, [(g, s + i * CAP) for g, s, lo, hi in adds if lo <= i < hi])
            for i in range(NZ)
        ]

    uc, ud = up_terms(
        (4,), (), (8, 8), [(0, 4, YD[i], i // 2, (i % 2) * CAP, ()) for i in range(NY)]
    )
    dc, dd = down_terms(
        (2,), (), (16, 16), [(0, ZD[i], 2, i // 4, (i % 4) * CAP, ()) for i in range(NZ)]
    )
    uc, ud = shift_fsdp(uc, 1, 0), shift_fsdp(ud, -1, 0)
    dc, dd = shift_fsdp(dc, 0, 1), shift_fsdp(dd, 0, -1)
    uc, ud = up_terms(
        (3, -3), (uc, ud), (16, 16),
        z_terms(0, 3, 0, [(0, 0, 0, 2)]) + z_terms(1, -3, 1, [(1, -8, 2, 4)]),
    )
    dc, dd = down_terms(
        (1, -1), (dc, dd), (32, 32),
        y_terms(0, 1, 0, [(0, 0, 0, 4)]) + y_terms(1, -1, 1, [(1, -16, 4, 8)]),
    )
    uc, ud = shift_fsdp(uc, 1, 0), shift_fsdp(ud, -1, 0)
    dc, dd = shift_fsdp(dc, 0, 1), shift_fsdp(dd, 0, -1)
    for k in (2, 1):
        uc, ud = up_terms(
            (k, -k), (uc, ud), (16, 16),
            z_terms(0, k, 0, [(0, 0, 0, 4)]) + z_terms(1, -k, 1, [(1, 0, 0, 4)]),
        )
        uc, ud = shift_fsdp(uc, 1, 0), shift_fsdp(ud, -1, 0)
    up_parts = up_terms(
        (0,), (uc, ud), (4,) * NY,
        [(0, 0, YD[i], i, 0, ((0, i * CAP), (1, i * CAP))) for i in range(NY)],
    )
    down_parts = down_terms(
        (0,), (dc, dd), (4,) * NZ,
        [(0, ZD[i], 0, i, 0, ((0, i * CAP), (1, i * CAP))) for i in range(NZ)],
    )
    up_sum = [up_parts[0]] + [shift_fsdp(up_parts[i], 0, YD[i]) for i in range(1, NY)]
    down_sum = [down_parts[0]] + [shift_fsdp(down_parts[i], ZD[i], 0) for i in range(1, NZ)]
    grad_up = place_grads(meta, up_cols, up_sum)
    grad_down = place_grads(meta, down_cols, down_sum)

    layer = project(
        meta, down_cols, active, (dn, dc1, dd1, dc2, dd2),
        [(i, j * CAP, ZD[j], YD[i]) for i in range(3) for j in range(NZ)]
        + [(3 + j // 4, (j % 4) * CAP, ZD[j], 2) for j in range(NZ)],
    )
    inputs = project(
        meta, up_cols, grad_hidden, (u, ua1, ub1, ua2, ub2, ua3, ub3, ua4, ub4),
        [(i, j * CAP, ZD[i], YD[j]) for i in range(7) for j in range(NY)]
        + [(7 + j // 2, (j % 2) * CAP, 4, YD[j]) for j in range(NY)],
    )
    mixed = reduce_features(*layer)
    grad_tokens = reduce_features(*inputs)
    return (mixed, grad_tokens, grad_up, grad_down)


def solution(mesh):
    return jax.shard_map(
        body,
        mesh=mesh,
        in_specs=(
            P("fsdp", "tp"),
            P("fsdp", "tp"),
            P("fsdp", "tp"),
            P("fsdp", "tp"),
            P("tp", None, None),
            P("tp"),
            P("tp", None, None),
            P("tp"),
        ),
        out_specs=(P("fsdp", "tp"), P("fsdp", "tp"), P("fsdp", "tp"), P("fsdp", "tp")),
        check_vma=False,
    )
```

```python
import jax
import jax.numpy as jnp
from jax import lax
from jax.experimental import pallas as pl
from jax.experimental.pallas import tpu as pltpu
from jax.sharding import PartitionSpec as P


BLK = 128
CAP = 4
NZ, NY, NX = 8, 4, 4
FBT = 14
TOK = 256
FEAT = NY * BLK

SQRT_TWO_PI = 0.7978845608028654
CUBIC = 0.044715

ZD = (0, -1, 1, -2, 2, -3, 3, 4)
YD = (0, -1, 1, 2)

BF16 = jnp.bfloat16
F32 = jnp.float32

VMEM_LIMIT = 24 << 20


def shift_fsdp(value, dz, dy):
    pairs = []
    for z in range(NZ):
        for y in range(NY):
            pairs.append((z * NY + y, ((z + dz) % NZ) * NY + (y + dy) % NY))
    return lax.ppermute(value, "fsdp", pairs)


def shift_x(value, dx):
    return lax.ppermute(value, "tp", [(i, (i + 2 * dx) % 8) for i in range(8)])


def partner(value):
    return lax.ppermute(value, "tp", [(i, i ^ 1) for i in range(8)])


def z_at(meta, i):
    return meta[4 + i]


def y_at(meta, i):
    return meta[12 + i]


def lanes(index):
    return pl.ds(pl.multiple_of(index * BLK, BLK), BLK)


def read_features(halves, which, meta, zz, yy):
    place = (meta[2] - (zz >> 1)) & (NX - 1)
    mine = halves[0][place, which, :, lanes(yy)]
    theirs = halves[1][place, which, :, lanes(yy)]
    return jnp.where((zz & 1) == meta[3], mine, theirs)


def row_at(meta, kind, offset, i):
    if kind == "z":
        return z_at(meta, ZD.index(offset)), y_at(meta, i)
    return z_at(meta, i), y_at(meta, YD.index(offset))


def slot_cols(cols, zz, yy):
    base = (zz * NY + yy) * CAP
    return [jnp.maximum(cols[base + j], 0) for j in range(CAP)]


def for_rows(low, high, step):
    if high - low <= 2:
        for i in range(low, high):
            step(i)
        return

    def turn(k, carry):
        step(low + 2 * k)
        step(low + 2 * k + 1)
        return carry

    lax.fori_loop(0, (high - low) // 2, turn, 0)


def call(kernel, tables, operands, outs, aliases=None, scratch=(), space=pltpu.VMEM):
    vmem = pl.BlockSpec(memory_space=pltpu.VMEM)
    return pl.pallas_call(
        kernel,
        out_shape=outs,
        in_specs=[pl.BlockSpec(memory_space=pltpu.SMEM)] * len(tables)
        + [pl.BlockSpec(memory_space=space)] * len(operands),
        out_specs=(vmem,) * len(outs) if isinstance(outs, tuple) else vmem,
        scratch_shapes=scratch,
        input_output_aliases=aliases or {},
        compiler_params=pltpu.CompilerParams(vmem_limit_bytes=VMEM_LIMIT),
    )(*tables, *operands)


def shaped(shape, dtype=BF16):
    return jax.ShapeDtypeStruct(shape, dtype)


def pick(meta, both_cols, up_weight, down_weight, tokens, cotangent):
    def kernel(meta, cols, up_ref, down_ref, x_ref, dy_ref, up_out, down_out, both_out, sems):
        base = (meta[0] * NY + meta[1]) * CAP
        copies = [
            pltpu.make_async_copy(x_ref, both_out.at[0], sems.at[0]),
            pltpu.make_async_copy(dy_ref, both_out.at[1], sems.at[1]),
        ]
        blocks = []
        for part, (source, target) in enumerate(((up_ref, up_out), (down_ref, down_out))):
            for j in range(CAP):
                col = cols[part, base + j]
                blocks.append((col, target, j))
                copies.append(
                    pltpu.make_async_copy(
                        source.at[:, lanes(jnp.maximum(col, 0))],
                        target.at[j],
                        sems.at[2 + part * CAP + j],
                    )
                )
        for copy in copies:
            copy.start()
        for copy in copies:
            copy.wait()
        for col, target, j in blocks:

            @pl.when(col < 0)
            def _():
                target[j] = jnp.zeros((BLK, BLK), BF16)

    block = (CAP, BLK, BLK)
    both = (2, TOK, FEAT)
    return call(
        kernel,
        (meta, both_cols),
        (up_weight, down_weight, tokens, cotangent),
        (shaped(block), shaped(block), shaped(both)),
        scratch=(pltpu.SemaphoreType.DMA((2 + 2 * CAP,)),),
        space=pltpu.HBM,
    )


def join(meta, pieces):
    sizes = [p.shape[0] for p in pieces]
    shape = (sum(sizes),) + pieces[0].shape[1:]

    def kernel(meta, *refs):
        at = 0
        for ref, size in zip(refs[:-1], sizes):
            refs[-1][at : at + size] = ref[...]
            at += size

    return call(kernel, (meta,), pieces, shaped(shape))


def add_products(meta, cols, which, segment, halves, chunk_refs, out):
    kind, offset, ci, low, high = segment

    def step(i):
        zz, yy = row_at(meta, kind, offset, i)
        left = read_features(halves, which, meta, zz, yy)
        base = (i - low) * CAP
        right = jnp.concatenate([chunk_refs[ci][base + j] for j in range(CAP)], axis=1)
        product = jnp.dot(left, right, preferred_element_type=F32)
        for j, col in enumerate(slot_cols(cols, zz, yy)):
            out[col] += product[:, j * BLK : (j + 1) * BLK]

    for_rows(low, high, step)


def accumulate(meta, cols, which, halves, chunks, segments, acc):
    def kernel(meta, cols, *refs):
        out = refs[-1]
        if acc is None:
            out[...] = jnp.zeros_like(out)
        for segment in segments:
            add_products(meta, cols, which, segment, refs[:2], refs[2:], out)

    operands = [*halves, *chunks]
    aliases = {}
    if acc is not None:
        operands.append(acc)
        aliases = {1 + len(operands): 0}
    return call(kernel, (meta, cols), operands, shaped((FBT, TOK, BLK), F32), aliases)


def finish(meta, up_cols, down_cols, halves, ups, downs, hidden, grad_active):
    def kernel(meta, up_cols, down_cols, own, other, *refs):
        up_refs, down_refs = refs[:2], refs[2:4]
        h_ref, g_ref, act_t, grad_t, h, g = refs[4:]
        h[...] = h_ref[...]
        g[...] = g_ref[...]
        for k in range(2):
            add_products(
                meta, up_cols, 0, ("z", 4, k, 2 * k, 2 * k + 2), (own, other), up_refs, h
            )
            add_products(
                meta, down_cols, 1, ("y", 2, k, 4 * k, 4 * k + 4), (own, other), down_refs, g
            )

        def step(c, carry):
            v = h[c]
            tangent = jnp.tanh(SQRT_TWO_PI * (v + CUBIC * v * v * v))
            slope = 0.5 * (1.0 + tangent) + 0.5 * v * (1.0 - tangent * tangent) * SQRT_TWO_PI * (
                1.0 + 3.0 * CUBIC * v * v
            )
            act_t[c] = (0.5 * v * (1.0 + tangent)).astype(BF16).T
            grad_t[c] = (g[c] * slope).astype(BF16).T
            return carry

        lax.fori_loop(0, FBT, step, 0)

    shape = (FBT, BLK, TOK)
    acc = pltpu.VMEM((FBT, TOK, BLK), F32)
    return call(
        kernel,
        (meta, up_cols, down_cols),
        (*halves, *ups, *downs, hidden, grad_active),
        (shaped(shape), shaped(shape)),
        scratch=(acc, acc),
    )


def terms(meta, cols, kind, which, units_t, halves, offsets, received, sizes, segments):
    def kernel(meta, cols, own, other, units, *refs):
        got, outs = refs[: len(received)], refs[len(received) :]
        for oi, low, high, to, first, adds in segments:

            def step(i):
                zz, yy = row_at(meta, kind, offsets[oi], i)
                right = read_features((own, other), which, meta, zz, yy)
                left = jnp.concatenate([units[c] for c in slot_cols(cols, zz, yy)], axis=0)
                product = jnp.dot(left, right, preferred_element_type=F32)
                total = product.reshape(CAP, BLK, BLK)
                for gi, start in adds:
                    total = total + got[gi][pl.ds((i - start) * CAP, CAP)].astype(F32)
                outs[to][pl.ds((i - first) * CAP, CAP)] = total.astype(BF16)

            for_rows(low, high, step)

    return call(
        kernel,
        (meta, cols),
        [*halves, units_t, *received],
        tuple(shaped((size * CAP, BLK, BLK)) for size in sizes),
    )


def project(meta, cols, kind, units_t, chunks, segments):
    def kernel(meta, cols, units, *refs):
        chunk_refs, (same, other) = refs[: len(chunks)], refs[len(chunks) :]
        for offset, ci, low, high in segments:

            def step(i):
                base = (i - low) * CAP
                left = jnp.concatenate([chunk_refs[ci][base + j] for j in range(CAP)], axis=1)
                zz, yy = row_at(meta, kind, offset, i)
                right = jnp.concatenate([units[c] for c in slot_cols(cols, zz, yy)], axis=0)
                product = jnp.dot(left, right, preferred_element_type=F32).astype(BF16)
                place = ((zz >> 1) - meta[2]) & (NX - 1)
                mine = (zz & 1) == meta[3]

                @pl.when(mine)
                def _():
                    same[place, yy] = product

                @pl.when(jnp.logical_not(mine))
                def _():
                    other[place, yy] = product

            for_rows(low, high, step)

    shape = (NX, NY, BLK, TOK)
    return call(kernel, (meta, cols), [units_t] + list(chunks), (shaped(shape), shaped(shape)))


def pair_sums(meta, pairs):
    def kernel(meta, *refs):
        outs = refs[2 * len(pairs) :]
        for p in range(len(pairs)):
            for k in range(NX):
                total = refs[2 * p][k].astype(F32) + refs[2 * p + 1][k].astype(F32)
                outs[k][p] = total.astype(BF16)

    out = shaped((len(pairs), NY, BLK, TOK))
    return call(kernel, (meta,), [a for pair in pairs for a in pair], (out,) * NX)


def final_sums(meta, pieces):
    def kernel(meta, *refs):
        sources, outs = refs[: len(pieces)], refs[len(pieces) :]
        for p, out in enumerate(outs):
            for k in range(NY):
                total = sources[0][p, k].astype(F32)
                for ref in sources[1:]:
                    total = total + ref[p, k].astype(F32)
                out[:, k * BLK : (k + 1) * BLK] = total.astype(BF16).T

    out = shaped((TOK, FEAT))
    return call(kernel, (meta,), pieces, (out,) * pieces[0].shape[0])


def place_grads(meta, cols, pieces):
    def kernel(meta, cols, *refs):
        out = refs[-1]
        out[...] = jnp.zeros_like(out)
        base = (meta[0] * NY + meta[1]) * CAP
        for j in range(CAP):
            total = refs[0][j].astype(F32)
            for ref in refs[1:-1]:
                total = total + ref[j].astype(F32)
            col = cols[base + j]

            @pl.when(col >= 0)
            def _():
                out[:, lanes(jnp.maximum(col, 0))] = total.T

    shape = (BLK, FBT * BLK)
    return call(kernel, (meta, cols), pieces, shaped(shape, F32))


def column_tables(lists, counts):
    rows, cols = lists[:, :, 0], lists[:, :, 1]
    index = jnp.arange(lists.shape[1], dtype=jnp.int32)
    valid = index[None, :] < counts[:, None]
    rows = jnp.where(valid, rows, -1)
    same = (rows[:, :, None] == rows[:, None, :]) & (index[None, None, :] < index[None, :, None])
    rank = jnp.sum(same.astype(jnp.int32), axis=2)
    slot = jnp.where(valid, rows * CAP + rank, -1)
    chosen = slot[:, None, :] == index[None, :, None]
    return jnp.sum(jnp.where(chosen, cols[:, None, :] + 1, 0), axis=2) - 1


def body(tokens, cotangent, up_weight, down_weight, up_list, up_count, down_list, down_count):
    group, slice_id = lax.axis_index("fsdp"), lax.axis_index("tp")
    z, y = group // NY, group % NY
    meta = jnp.concatenate(
        [
            jnp.stack([z, y, slice_id // 2, slice_id % 2]),
            (z + jnp.array(ZD, jnp.int32)) & (NZ - 1),
            (y + jnp.array(YD, jnp.int32)) & (NY - 1),
        ]
    ).astype(jnp.int32)
    tables = column_tables(
        jnp.concatenate([up_list, down_list]), jnp.concatenate([up_count, down_count])
    )
    up_cols, down_cols = tables[0], tables[1]
    up_own, down_own, local = pick(meta, tables, up_weight, down_weight, tokens, cotangent)

    up_near = [shift_fsdp(up_own, 0, -d) for d in YD[1:]]
    da1, db1 = shift_fsdp(down_own, 1, 0), shift_fsdp(down_own, -1, 0)
    far = [shift_x(local, k) for k in (1, 2, 3)]
    u = join(meta, [up_own] + up_near)
    ua1, ub1 = shift_fsdp(u, 1, 0), shift_fsdp(u, -1, 0)
    da2, db2 = shift_fsdp(da1, 1, 0), shift_fsdp(db1, -1, 0)
    da3, db3 = shift_fsdp(da2, 1, 0), shift_fsdp(db2, -1, 0)
    da4 = shift_fsdp(da3, 1, 0)
    ua2, ub2 = shift_fsdp(ua1, 1, 0), shift_fsdp(ub1, -1, 0)
    dn = join(meta, [down_own, da1, db1, da2, db2, da3, db3, da4])
    dc1, dd1 = shift_fsdp(dn, 0, 1), shift_fsdp(dn, 0, -1)
    half = join(meta, [a[None] for a in (local, *far)])
    halves = (half, partner(half))
    ua3, ub3 = shift_fsdp(ua2, 1, 0), shift_fsdp(ub2, -1, 0)
    dc2 = shift_fsdp(lax.slice_in_dim(dc1, 0, 16), 0, 1)
    dd2 = shift_fsdp(lax.slice_in_dim(dd1, 16, 32), 0, -1)
    ua4 = shift_fsdp(lax.slice_in_dim(ua3, 0, 8), 1, 0)
    ub4 = shift_fsdp(lax.slice_in_dim(ub3, 8, 16), -1, 0)

    hidden = accumulate(
        meta, up_cols, 0, halves, (u, ua1, ub1),
        [("z", 0, 0, 0, 4), ("z", -1, 1, 0, 4), ("z", 1, 2, 0, 4)], None,
    )
    grad_active = accumulate(meta, down_cols, 1, halves, (dn,), [("y", 0, 0, 0, 8)], None)
    hidden = accumulate(
        meta, up_cols, 0, halves, (ua2, ub2),
        [("z", -2, 0, 0, 4), ("z", 2, 1, 0, 4)], hidden,
    )
    grad_active = accumulate(
        meta, down_cols, 1, halves, (dc1, dd1),
        [("y", -1, 0, 0, 8), ("y", 1, 1, 0, 8)], grad_active,
    )
    hidden = accumulate(
        meta, up_cols, 0, halves, (ua3, ub3),
        [("z", -3, 0, 0, 4), ("z", 3, 1, 0, 4)], hidden,
    )
    active_t, grad_hidden_t = finish(
        meta, up_cols, down_cols, halves, (ua4, ub4), (dc2, dd2), hidden, grad_active
    )

    def up_terms(offsets, received, sizes, segments):
        return terms(
            meta, up_cols, "z", 0, grad_hidden_t, halves, offsets, received, sizes, segments
        )

    def down_terms(offsets, received, sizes, segments):
        return terms(meta, down_cols, "y", 1, active_t, halves, offsets, received, sizes, segments)

    def both_ways_z(pair):
        return shift_fsdp(pair[0], 1, 0), shift_fsdp(pair[1], -1, 0)

    def both_ways_y(pair):
        return shift_fsdp(pair[0], 0, 1), shift_fsdp(pair[1], 0, -1)

    down = both_ways_y(down_terms((2,), (), (4, 4), [(0, 0, 4, 0, 0, ()), (0, 4, 8, 1, 4, ())]))
    up = both_ways_z(up_terms((4,), (), (2, 2), [(0, 0, 2, 0, 0, ()), (0, 2, 4, 1, 2, ())]))
    layer = project(
        meta, down_cols, "y", active_t, (dn, dc1, dd1, dc2, dd2),
        [(0, 0, 0, 8), (-1, 1, 0, 8), (1, 2, 0, 8), (2, 3, 0, 4), (2, 4, 4, 8)],
    )
    layer = (layer[0], partner(layer[1]))
    up = both_ways_z(up_terms(
        (3, -3), up, (4, 4),
        [(0, 0, 2, 0, 0, ((0, 0),)), (0, 2, 4, 0, 0, ()),
         (1, 0, 2, 1, 0, ()), (1, 2, 4, 1, 0, ((1, 2),))],
    ))
    down = both_ways_y(down_terms(
        (1, -1), down, (8, 8),
        [(0, 0, 4, 0, 0, ((0, 0),)), (0, 4, 8, 0, 0, ()),
         (1, 0, 4, 1, 0, ()), (1, 4, 8, 1, 0, ((1, 4),))],
    ))
    inputs = project(
        meta, up_cols, "z", grad_hidden_t, (u, ua1, ub1, ua2, ub2, ua3, ub3, ua4, ub4),
        [(ZD[i], i, 0, 4) for i in range(7)] + [(4, 7, 0, 2), (4, 8, 2, 4)],
    )
    inputs = (inputs[0], partner(inputs[1]))
    for k in (2, 1):
        up = both_ways_z(up_terms(
            (k, -k), up, (4, 4), [(0, 0, 4, 0, 0, ((0, 0),)), (1, 0, 4, 1, 0, ((1, 0),))]
        ))
    pair = pair_sums(meta, [layer, inputs])
    down_parts = down_terms(
        (0,), down, (1,) * NZ, [(0, i, i + 1, i, i, ((0, 0), (1, 0))) for i in range(NZ)]
    )
    up_parts = up_terms(
        (0,), up, (1,) * NY, [(0, i, i + 1, i, i, ((0, 0), (1, 0))) for i in range(NY)]
    )
    down_pieces = [down_parts[0]] + [shift_fsdp(down_parts[i], ZD[i], 0) for i in range(1, NZ)]
    up_pieces = [up_parts[0]] + [shift_fsdp(up_parts[i], 0, YD[i]) for i in range(1, NY)]
    mixed, grad_tokens = final_sums(meta, [pair[0]] + [shift_x(pair[k], k) for k in (1, 2, 3)])
    grad_down = place_grads(meta, down_cols, down_pieces)
    grad_up = place_grads(meta, up_cols, up_pieces)
    return (mixed, grad_tokens, grad_up, grad_down)


def solution(mesh):
    return jax.shard_map(
        body,
        mesh=mesh,
        in_specs=(
            P("fsdp", "tp"),
            P("fsdp", "tp"),
            P("fsdp", "tp"),
            P("fsdp", "tp"),
            P("tp", None, None),
            P("tp"),
            P("tp", None, None),
            P("tp"),
        ),
        out_specs=(P("fsdp", "tp"), P("fsdp", "tp"), P("fsdp", "tp"), P("fsdp", "tp")),
        check_vma=False,
    )
```

```python
import jax
import jax.numpy as jnp
from jax import lax
from jax.experimental import pallas as pl
from jax.experimental.pallas import tpu as pltpu
from jax.sharding import PartitionSpec as P


BLK = 128
CAP = 4
NZ, NY, NX = 8, 4, 4
FBT = 14
TOK = 256
FEAT = NY * BLK

SQRT_TWO_PI = 0.7978845608028654
CUBIC = 0.044715

ZD = (0, -1, 1, -2, 2, -3, 3, 4)
YD = (0, -1, 1, 2)

BF16 = jnp.bfloat16
F32 = jnp.float32

VMEM_LIMIT = 24 << 20


def shift_fsdp(value, dz, dy):
    pairs = []
    for z in range(NZ):
        for y in range(NY):
            pairs.append((z * NY + y, ((z + dz) % NZ) * NY + (y + dy) % NY))
    return lax.ppermute(value, "fsdp", pairs)


def shift_x(value, dx):
    return lax.ppermute(value, "tp", [(i, (i + 2 * dx) % 8) for i in range(8)])


def partner(value):
    return lax.ppermute(value, "tp", [(i, i ^ 1) for i in range(8)])


def z_at(meta, i):
    return meta[4 + i]


def y_at(meta, i):
    return meta[12 + i]


def lanes(index):
    return pl.ds(pl.multiple_of(index * BLK, BLK), BLK)


def read_features(halves, which, meta, zz, yy):
    place = (meta[2] - (zz >> 1)) & (NX - 1)
    mine = halves[0][place, which, :, lanes(yy)]
    theirs = halves[1][place, which, :, lanes(yy)]
    return jnp.where((zz & 1) == meta[3], mine, theirs)


def row_at(meta, kind, offset, i):
    if kind == "z":
        return z_at(meta, ZD.index(offset)), y_at(meta, i)
    return z_at(meta, i), y_at(meta, YD.index(offset))


def slot_cols(cols, zz, yy):
    base = (zz * NY + yy) * CAP
    return [jnp.maximum(cols[base + j], 0) for j in range(CAP)]


def for_rows(low, high, step):
    if high - low <= 2:
        for i in range(low, high):
            step(i)
        return

    def turn(k, carry):
        step(low + 2 * k)
        step(low + 2 * k + 1)
        return carry

    lax.fori_loop(0, (high - low) // 2, turn, 0)


def call(kernel, tables, operands, outs, aliases=None, scratch=(), space=pltpu.VMEM):
    vmem = pl.BlockSpec(memory_space=pltpu.VMEM)
    return pl.pallas_call(
        kernel,
        out_shape=outs,
        in_specs=[pl.BlockSpec(memory_space=pltpu.SMEM)] * len(tables)
        + [pl.BlockSpec(memory_space=space)] * len(operands),
        out_specs=(vmem,) * len(outs) if isinstance(outs, tuple) else vmem,
        scratch_shapes=scratch,
        input_output_aliases=aliases or {},
        compiler_params=pltpu.CompilerParams(vmem_limit_bytes=VMEM_LIMIT),
    )(*tables, *operands)


def shaped(shape, dtype=BF16):
    return jax.ShapeDtypeStruct(shape, dtype)


def pick(meta, both_cols, up_weight, down_weight, tokens, cotangent):
    def kernel(meta, cols, up_ref, down_ref, x_ref, dy_ref, up_out, down_out, both_out, sems):
        base = (meta[0] * NY + meta[1]) * CAP
        copies = [
            pltpu.make_async_copy(x_ref, both_out.at[0], sems.at[0]),
            pltpu.make_async_copy(dy_ref, both_out.at[1], sems.at[1]),
        ]
        blocks = []
        for part, (source, target) in enumerate(((up_ref, up_out), (down_ref, down_out))):
            for j in range(CAP):
                col = cols[part, base + j]
                blocks.append((col, target, j))
                copies.append(
                    pltpu.make_async_copy(
                        source.at[:, lanes(jnp.maximum(col, 0))],
                        target.at[j],
                        sems.at[2 + part * CAP + j],
                    )
                )
        for copy in copies:
            copy.start()
        for copy in copies:
            copy.wait()
        for col, target, j in blocks:

            @pl.when(col < 0)
            def _():
                target[j] = jnp.zeros((BLK, BLK), BF16)

    block = (CAP, BLK, BLK)
    both = (2, TOK, FEAT)
    return call(
        kernel,
        (meta, both_cols),
        [
            pltpu.with_memory_space_constraint(a, pltpu.HBM)
            for a in (up_weight, down_weight, tokens, cotangent)
        ],
        (shaped(block), shaped(block), shaped(both)),
        scratch=(pltpu.SemaphoreType.DMA((2 + 2 * CAP,)),),
        space=pltpu.HBM,
    )


def join(meta, pieces):
    sizes = [p.shape[0] for p in pieces]
    shape = (sum(sizes),) + pieces[0].shape[1:]

    def kernel(meta, *refs):
        at = 0
        for ref, size in zip(refs[:-1], sizes):
            refs[-1][at : at + size] = ref[...]
            at += size

    return call(kernel, (meta,), pieces, shaped(shape))


def add_products(meta, cols, which, segment, halves, chunk_refs, out):
    kind, offset, ci, low, high = segment

    def step(i):
        zz, yy = row_at(meta, kind, offset, i)
        left = read_features(halves, which, meta, zz, yy)
        base = (i - low) * CAP
        right = jnp.concatenate([chunk_refs[ci][base + j] for j in range(CAP)], axis=1)
        product = jnp.dot(left, right, preferred_element_type=F32)
        for j, col in enumerate(slot_cols(cols, zz, yy)):
            out[col] += product[:, j * BLK : (j + 1) * BLK]

    for_rows(low, high, step)


def accumulate(meta, cols, which, halves, chunks, segments, acc):
    def kernel(meta, cols, *refs):
        out = refs[-1]
        if acc is None:
            out[...] = jnp.zeros_like(out)
        for segment in segments:
            add_products(meta, cols, which, segment, refs[:2], refs[2:], out)

    operands = [*halves, *chunks]
    aliases = {}
    if acc is not None:
        operands.append(acc)
        aliases = {1 + len(operands): 0}
    return call(kernel, (meta, cols), operands, shaped((FBT, TOK, BLK), F32), aliases)


def finish(meta, up_cols, down_cols, halves, ups, downs, hidden, grad_active):
    def kernel(meta, up_cols, down_cols, own, other, *refs):
        up_refs, down_refs = refs[:2], refs[2:4]
        h_ref, g_ref, act_t, grad_t, h, g = refs[4:]
        h[...] = h_ref[...]
        g[...] = g_ref[...]
        for k in range(2):
            add_products(
                meta, up_cols, 0, ("z", 4, k, 2 * k, 2 * k + 2), (own, other), up_refs, h
            )
            add_products(
                meta, down_cols, 1, ("y", 2, k, 4 * k, 4 * k + 4), (own, other), down_refs, g
            )

        def step(c, carry):
            v = h[c]
            tangent = jnp.tanh(SQRT_TWO_PI * (v + CUBIC * v * v * v))
            slope = 0.5 * (1.0 + tangent) + 0.5 * v * (1.0 - tangent * tangent) * SQRT_TWO_PI * (
                1.0 + 3.0 * CUBIC * v * v
            )
            act_t[c] = (0.5 * v * (1.0 + tangent)).astype(BF16).T
            grad_t[c] = (g[c] * slope).astype(BF16).T
            return carry

        lax.fori_loop(0, FBT, step, 0)

    shape = (FBT, BLK, TOK)
    acc = pltpu.VMEM((FBT, TOK, BLK), F32)
    return call(
        kernel,
        (meta, up_cols, down_cols),
        (*halves, *ups, *downs, hidden, grad_active),
        (shaped(shape), shaped(shape)),
        scratch=(acc, acc),
    )


def terms(meta, cols, kind, which, units_t, halves, offsets, received, sizes, segments):
    def kernel(meta, cols, own, other, units, *refs):
        got, outs = refs[: len(received)], refs[len(received) :]
        for oi, low, high, to, first, adds in segments:

            def step(i):
                zz, yy = row_at(meta, kind, offsets[oi], i)
                right = read_features((own, other), which, meta, zz, yy)
                left = jnp.concatenate([units[c] for c in slot_cols(cols, zz, yy)], axis=0)
                product = jnp.dot(left, right, preferred_element_type=F32)
                total = product.reshape(CAP, BLK, BLK)
                for gi, start in adds:
                    total = total + got[gi][pl.ds((i - start) * CAP, CAP)].astype(F32)
                outs[to][pl.ds((i - first) * CAP, CAP)] = total.astype(BF16)

            for_rows(low, high, step)

    return call(
        kernel,
        (meta, cols),
        [*halves, units_t, *received],
        tuple(shaped((size * CAP, BLK, BLK)) for size in sizes),
    )


def project(meta, cols, kind, units_t, chunks, segments):
    def kernel(meta, cols, units, *refs):
        chunk_refs, (same, other) = refs[: len(chunks)], refs[len(chunks) :]
        for offset, ci, low, high in segments:

            def step(i):
                base = (i - low) * CAP
                left = jnp.concatenate([chunk_refs[ci][base + j] for j in range(CAP)], axis=1)
                zz, yy = row_at(meta, kind, offset, i)
                right = jnp.concatenate([units[c] for c in slot_cols(cols, zz, yy)], axis=0)
                product = jnp.dot(left, right, preferred_element_type=F32).astype(BF16)
                place = ((zz >> 1) - meta[2]) & (NX - 1)
                mine = (zz & 1) == meta[3]

                @pl.when(mine)
                def _():
                    same[place, yy] = product

                @pl.when(jnp.logical_not(mine))
                def _():
                    other[place, yy] = product

            for_rows(low, high, step)

    shape = (NX, NY, BLK, TOK)
    return call(kernel, (meta, cols), [units_t] + list(chunks), (shaped(shape), shaped(shape)))


def pair_sums(meta, pairs):
    def kernel(meta, *refs):
        outs = refs[2 * len(pairs) :]
        for p in range(len(pairs)):
            for k in range(NX):
                total = refs[2 * p][k].astype(F32) + refs[2 * p + 1][k].astype(F32)
                outs[k][p] = total.astype(BF16)

    out = shaped((len(pairs), NY, BLK, TOK))
    return call(kernel, (meta,), [a for pair in pairs for a in pair], (out,) * NX)


def final_sums(meta, pieces):
    def kernel(meta, *refs):
        sources, outs = refs[: len(pieces)], refs[len(pieces) :]
        for p, out in enumerate(outs):
            for k in range(NY):
                total = sources[0][p, k].astype(F32)
                for ref in sources[1:]:
                    total = total + ref[p, k].astype(F32)
                out[:, k * BLK : (k + 1) * BLK] = total.astype(BF16).T

    out = shaped((TOK, FEAT))
    return call(kernel, (meta,), pieces, (out,) * pieces[0].shape[0])


def place_grads(meta, cols, pieces):
    def kernel(meta, cols, *refs):
        out = refs[-1]
        out[...] = jnp.zeros_like(out)
        base = (meta[0] * NY + meta[1]) * CAP
        for j in range(CAP):
            total = refs[0][j].astype(F32)
            for ref in refs[1:-1]:
                total = total + ref[j].astype(F32)
            col = cols[base + j]

            @pl.when(col >= 0)
            def _():
                out[:, lanes(jnp.maximum(col, 0))] = total.T

    shape = (BLK, FBT * BLK)
    return call(kernel, (meta, cols), pieces, shaped(shape, F32))


def column_tables(lists, counts):
    rows, cols = lists[:, :, 0], lists[:, :, 1]
    index = jnp.arange(lists.shape[1], dtype=jnp.int32)
    valid = index[None, :] < counts[:, None]
    rows = jnp.where(valid, rows, -1)
    same = (rows[:, :, None] == rows[:, None, :]) & (index[None, None, :] < index[None, :, None])
    rank = jnp.sum(same.astype(jnp.int32), axis=2)
    slot = jnp.where(valid, rows * CAP + rank, -1)
    chosen = slot[:, None, :] == index[None, :, None]
    return jnp.sum(jnp.where(chosen, cols[:, None, :] + 1, 0), axis=2) - 1


def body(tokens, cotangent, up_weight, down_weight, up_list, up_count, down_list, down_count):
    group, slice_id = lax.axis_index("fsdp"), lax.axis_index("tp")
    z, y = group // NY, group % NY
    meta = jnp.concatenate(
        [
            jnp.stack([z, y, slice_id // 2, slice_id % 2]),
            (z + jnp.array(ZD, jnp.int32)) & (NZ - 1),
            (y + jnp.array(YD, jnp.int32)) & (NY - 1),
        ]
    ).astype(jnp.int32)
    tables = column_tables(
        jnp.concatenate([up_list, down_list]), jnp.concatenate([up_count, down_count])
    )
    up_cols, down_cols = tables[0], tables[1]
    up_own, down_own, local = pick(meta, tables, up_weight, down_weight, tokens, cotangent)

    up_near = [shift_fsdp(up_own, 0, -d) for d in YD[1:]]
    da1, db1 = shift_fsdp(down_own, 1, 0), shift_fsdp(down_own, -1, 0)
    far = [shift_x(local, k) for k in (1, 2, 3)]
    u = join(meta, [up_own] + up_near)
    ua1, ub1 = shift_fsdp(u, 1, 0), shift_fsdp(u, -1, 0)
    da2, db2 = shift_fsdp(da1, 1, 0), shift_fsdp(db1, -1, 0)
    da3, db3 = shift_fsdp(da2, 1, 0), shift_fsdp(db2, -1, 0)
    da4 = shift_fsdp(da3, 1, 0)
    ua2, ub2 = shift_fsdp(ua1, 1, 0), shift_fsdp(ub1, -1, 0)
    dn = join(meta, [down_own, da1, db1, da2, db2, da3, db3, da4])
    dc1, dd1 = shift_fsdp(dn, 0, 1), shift_fsdp(dn, 0, -1)
    half = join(meta, [a[None] for a in (local, *far)])
    halves = (half, partner(half))
    ua3, ub3 = shift_fsdp(ua2, 1, 0), shift_fsdp(ub2, -1, 0)
    dc2 = shift_fsdp(lax.slice_in_dim(dc1, 0, 16), 0, 1)
    dd2 = shift_fsdp(lax.slice_in_dim(dd1, 16, 32), 0, -1)
    ua4 = shift_fsdp(lax.slice_in_dim(ua3, 0, 8), 1, 0)
    ub4 = shift_fsdp(lax.slice_in_dim(ub3, 8, 16), -1, 0)

    hidden = accumulate(
        meta, up_cols, 0, halves, (u, ua1, ub1),
        [("z", 0, 0, 0, 4), ("z", -1, 1, 0, 4), ("z", 1, 2, 0, 4)], None,
    )
    grad_active = accumulate(meta, down_cols, 1, halves, (dn,), [("y", 0, 0, 0, 8)], None)
    hidden = accumulate(
        meta, up_cols, 0, halves, (ua2, ub2),
        [("z", -2, 0, 0, 4), ("z", 2, 1, 0, 4)], hidden,
    )
    grad_active = accumulate(
        meta, down_cols, 1, halves, (dc1, dd1),
        [("y", -1, 0, 0, 8), ("y", 1, 1, 0, 8)], grad_active,
    )
    hidden = accumulate(
        meta, up_cols, 0, halves, (ua3, ub3),
        [("z", -3, 0, 0, 4), ("z", 3, 1, 0, 4)], hidden,
    )
    active_t, grad_hidden_t = finish(
        meta, up_cols, down_cols, halves, (ua4, ub4), (dc2, dd2), hidden, grad_active
    )

    def up_terms(offsets, received, sizes, segments):
        return terms(
            meta, up_cols, "z", 0, grad_hidden_t, halves, offsets, received, sizes, segments
        )

    def down_terms(offsets, received, sizes, segments):
        return terms(meta, down_cols, "y", 1, active_t, halves, offsets, received, sizes, segments)

    def both_ways_z(pair):
        return shift_fsdp(pair[0], 1, 0), shift_fsdp(pair[1], -1, 0)

    def both_ways_y(pair):
        return shift_fsdp(pair[0], 0, 1), shift_fsdp(pair[1], 0, -1)

    down = both_ways_y(down_terms((2,), (), (4, 4), [(0, 0, 4, 0, 0, ()), (0, 4, 8, 1, 4, ())]))
    up = both_ways_z(up_terms((4,), (), (2, 2), [(0, 0, 2, 0, 0, ()), (0, 2, 4, 1, 2, ())]))
    layer = project(
        meta, down_cols, "y", active_t, (dn, dc1, dd1, dc2, dd2),
        [(0, 0, 0, 8), (-1, 1, 0, 8), (1, 2, 0, 8), (2, 3, 0, 4), (2, 4, 4, 8)],
    )
    layer = (layer[0], partner(layer[1]))
    up = both_ways_z(up_terms(
        (3, -3), up, (4, 4),
        [(0, 0, 2, 0, 0, ((0, 0),)), (0, 2, 4, 0, 0, ()),
         (1, 0, 2, 1, 0, ()), (1, 2, 4, 1, 0, ((1, 2),))],
    ))
    down = both_ways_y(down_terms(
        (1, -1), down, (8, 8),
        [(0, 0, 4, 0, 0, ((0, 0),)), (0, 4, 8, 0, 0, ()),
         (1, 0, 4, 1, 0, ()), (1, 4, 8, 1, 0, ((1, 4),))],
    ))
    inputs = project(
        meta, up_cols, "z", grad_hidden_t, (u, ua1, ub1, ua2, ub2, ua3, ub3, ua4, ub4),
        [(ZD[i], i, 0, 4) for i in range(7)] + [(4, 7, 0, 2), (4, 8, 2, 4)],
    )
    inputs = (inputs[0], partner(inputs[1]))
    for k in (2, 1):
        up = both_ways_z(up_terms(
            (k, -k), up, (4, 4), [(0, 0, 4, 0, 0, ((0, 0),)), (1, 0, 4, 1, 0, ((1, 0),))]
        ))
    pair = pair_sums(meta, [layer, inputs])
    down_parts = down_terms(
        (0,), down, (1,) * NZ, [(0, i, i + 1, i, i, ((0, 0), (1, 0))) for i in range(NZ)]
    )
    up_parts = up_terms(
        (0,), up, (1,) * NY, [(0, i, i + 1, i, i, ((0, 0), (1, 0))) for i in range(NY)]
    )
    down_pieces = [down_parts[0]] + [shift_fsdp(down_parts[i], ZD[i], 0) for i in range(1, NZ)]
    up_pieces = [up_parts[0]] + [shift_fsdp(up_parts[i], 0, YD[i]) for i in range(1, NY)]
    mixed, grad_tokens = final_sums(meta, [pair[0]] + [shift_x(pair[k], k) for k in (1, 2, 3)])
    grad_down = place_grads(meta, down_cols, down_pieces)
    grad_up = place_grads(meta, up_cols, up_pieces)
    return (mixed, grad_tokens, grad_up, grad_down)


def solution(mesh):
    return jax.shard_map(
        body,
        mesh=mesh,
        in_specs=(
            P("fsdp", "tp"),
            P("fsdp", "tp"),
            P("fsdp", "tp"),
            P("fsdp", "tp"),
            P("tp", None, None),
            P("tp"),
            P("tp", None, None),
            P("tp"),
        ),
        out_specs=(P("fsdp", "tp"), P("fsdp", "tp"), P("fsdp", "tp"), P("fsdp", "tp")),
        check_vma=False,
    )
```

```python
import jax
import jax.numpy as jnp
from jax import lax
from jax.experimental import pallas as pl
from jax.experimental.pallas import tpu as pltpu
from jax.sharding import PartitionSpec as P


BLK = 128
CAP = 4
NZ, NY, NX = 8, 4, 4
FBT = 14
TOK = 256
FEAT = NY * BLK

SQRT_TWO_PI = 0.7978845608028654
CUBIC = 0.044715

ZD = (0, -1, 1, -2, 2, -3, 3, 4)
YD = (0, -1, 1, 2)

BF16 = jnp.bfloat16
F32 = jnp.float32

VMEM_LIMIT = 24 << 20


def shift_fsdp(value, dz, dy):
    pairs = []
    for z in range(NZ):
        for y in range(NY):
            pairs.append((z * NY + y, ((z + dz) % NZ) * NY + (y + dy) % NY))
    return lax.ppermute(value, "fsdp", pairs)


def shift_x(value, dx):
    return lax.ppermute(value, "tp", [(i, (i + 2 * dx) % 8) for i in range(8)])


def partner(value):
    return lax.ppermute(value, "tp", [(i, i ^ 1) for i in range(8)])


def z_at(meta, i):
    return meta[4 + i]


def y_at(meta, i):
    return meta[12 + i]


def lanes(index):
    return pl.ds(pl.multiple_of(index * BLK, BLK), BLK)


def read_features(halves, which, meta, zz, yy):
    place = (meta[2] - (zz >> 1)) & (NX - 1)
    mine = halves[0][place, which, :, lanes(yy)]
    theirs = halves[1][place, which, :, lanes(yy)]
    return jnp.where((zz & 1) == meta[3], mine, theirs)


def row_at(meta, kind, offset, i):
    if kind == "z":
        return z_at(meta, ZD.index(offset)), y_at(meta, i)
    return z_at(meta, i), y_at(meta, YD.index(offset))


def slot_cols(cols, zz, yy):
    base = (zz * NY + yy) * CAP
    return [jnp.maximum(cols[base + j], 0) for j in range(CAP)]


def for_rows(low, high, step):
    if high - low <= 2:
        for i in range(low, high):
            step(i)
        return

    def turn(k, carry):
        step(low + 2 * k)
        step(low + 2 * k + 1)
        return carry

    lax.fori_loop(0, (high - low) // 2, turn, 0)


def call(kernel, tables, operands, outs, aliases=None, scratch=(), space=pltpu.VMEM):
    vmem = pl.BlockSpec(memory_space=pltpu.VMEM)
    return pl.pallas_call(
        kernel,
        out_shape=outs,
        in_specs=[pl.BlockSpec(memory_space=pltpu.SMEM)] * len(tables)
        + [pl.BlockSpec(memory_space=space)] * len(operands),
        out_specs=(vmem,) * len(outs) if isinstance(outs, tuple) else vmem,
        scratch_shapes=scratch,
        input_output_aliases=aliases or {},
        compiler_params=pltpu.CompilerParams(vmem_limit_bytes=VMEM_LIMIT),
    )(*tables, *operands)


def shaped(shape, dtype=BF16):
    return jax.ShapeDtypeStruct(shape, dtype)


def pick(meta, both_cols, up_weight, down_weight, tokens, cotangent):
    def kernel(meta, cols, up_ref, down_ref, x_ref, dy_ref, up_out, down_out, both_out, sems):
        base = (meta[0] * NY + meta[1]) * CAP
        copies = [
            pltpu.make_async_copy(x_ref, both_out.at[0], sems.at[0]),
            pltpu.make_async_copy(dy_ref, both_out.at[1], sems.at[1]),
        ]
        blocks = []
        for part, (source, target) in enumerate(((up_ref, up_out), (down_ref, down_out))):
            for j in range(CAP):
                col = cols[part, base + j]
                blocks.append((col, target, j))
                copies.append(
                    pltpu.make_async_copy(
                        source.at[:, lanes(jnp.maximum(col, 0))],
                        target.at[j],
                        sems.at[2 + part * CAP + j],
                    )
                )
        for copy in copies:
            copy.start()
        for copy in copies:
            copy.wait()
        for col, target, j in blocks:

            @pl.when(col < 0)
            def _():
                target[j] = jnp.zeros((BLK, BLK), BF16)

    block = (CAP, BLK, BLK)
    both = (2, TOK, FEAT)
    return call(
        kernel,
        (meta, both_cols),
        [
            pltpu.with_memory_space_constraint(a, pltpu.HBM)
            for a in (up_weight, down_weight, tokens, cotangent)
        ],
        (shaped(block), shaped(block), shaped(both)),
        scratch=(pltpu.SemaphoreType.DMA((2 + 2 * CAP,)),),
        space=pltpu.HBM,
    )


def join(meta, pieces):
    sizes = [p.shape[0] for p in pieces]
    shape = (sum(sizes),) + pieces[0].shape[1:]

    def kernel(meta, *refs):
        at = 0
        for ref, size in zip(refs[:-1], sizes):
            refs[-1][at : at + size] = ref[...]
            at += size

    return call(kernel, (meta,), pieces, shaped(shape))


def add_products(meta, cols, which, segment, halves, chunk_refs, out):
    kind, offset, ci, low, high = segment

    def step(i):
        zz, yy = row_at(meta, kind, offset, i)
        left = read_features(halves, which, meta, zz, yy)
        base = (i - low) * CAP
        right = jnp.concatenate([chunk_refs[ci][base + j] for j in range(CAP)], axis=1)
        product = jnp.dot(left, right, preferred_element_type=F32)
        for j, col in enumerate(slot_cols(cols, zz, yy)):
            out[col] += product[:, j * BLK : (j + 1) * BLK]

    for_rows(low, high, step)


def accumulate(meta, cols, which, halves, chunks, segments, acc):
    def kernel(meta, cols, *refs):
        out = refs[-1]
        if acc is None:
            out[...] = jnp.zeros_like(out)
        for segment in segments:
            add_products(meta, cols, which, segment, refs[:2], refs[2:], out)

    operands = [*halves, *chunks]
    aliases = {}
    if acc is not None:
        operands.append(acc)
        aliases = {1 + len(operands): 0}
    return call(kernel, (meta, cols), operands, shaped((FBT, TOK, BLK), F32), aliases)


def finish(meta, up_cols, down_cols, halves, ups, downs, hidden, grad_active):
    def kernel(meta, up_cols, down_cols, own, other, *refs):
        up_refs, down_refs = refs[:2], refs[2:4]
        act_t, grad_t, h, g = refs[6:]
        for k in range(2):
            add_products(
                meta, up_cols, 0, ("z", 4, k, 2 * k, 2 * k + 2), (own, other), up_refs, h
            )
            add_products(
                meta, down_cols, 1, ("y", 2, k, 4 * k, 4 * k + 4), (own, other), down_refs, g
            )

        def step(c, carry):
            v = h[c]
            tangent = jnp.tanh(SQRT_TWO_PI * (v + CUBIC * v * v * v))
            slope = 0.5 * (1.0 + tangent) + 0.5 * v * (1.0 - tangent * tangent) * SQRT_TWO_PI * (
                1.0 + 3.0 * CUBIC * v * v
            )
            act_t[c] = (0.5 * v * (1.0 + tangent)).astype(BF16).T
            grad_t[c] = (g[c] * slope).astype(BF16).T
            return carry

        lax.fori_loop(0, FBT, step, 0)

    shape = (FBT, BLK, TOK)
    sums = shaped(hidden.shape, F32)
    return call(
        kernel,
        (meta, up_cols, down_cols),
        (*halves, *ups, *downs, hidden, grad_active),
        (shaped(shape), shaped(shape), sums, sums),
        {9: 2, 10: 3},
    )[:2]


def terms(meta, cols, kind, which, units_t, halves, offsets, received, sizes, segments):
    def kernel(meta, cols, own, other, units, *refs):
        got, outs = refs[: len(received)], refs[len(received) :]
        for oi, low, high, to, first, adds in segments:

            def step(i):
                zz, yy = row_at(meta, kind, offsets[oi], i)
                right = read_features((own, other), which, meta, zz, yy)
                left = jnp.concatenate([units[c] for c in slot_cols(cols, zz, yy)], axis=0)
                product = jnp.dot(left, right, preferred_element_type=F32)
                total = product.reshape(CAP, BLK, BLK)
                for gi, start in adds:
                    total = total + got[gi][pl.ds((i - start) * CAP, CAP)].astype(F32)
                outs[to][pl.ds((i - first) * CAP, CAP)] = total.astype(BF16)

            for_rows(low, high, step)

    return call(
        kernel,
        (meta, cols),
        [*halves, units_t, *received],
        tuple(shaped((size * CAP, BLK, BLK)) for size in sizes),
    )


def project(meta, cols, kind, units_t, chunks, segments, begun=()):
    def kernel(meta, cols, units, *refs):
        chunk_refs, (same, other) = refs[: len(chunks)], refs[-2:]
        for offset, ci, low, high in segments:

            def step(i):
                base = (i - low) * CAP
                left = jnp.concatenate([chunk_refs[ci][base + j] for j in range(CAP)], axis=1)
                zz, yy = row_at(meta, kind, offset, i)
                right = jnp.concatenate([units[c] for c in slot_cols(cols, zz, yy)], axis=0)
                product = jnp.dot(left, right, preferred_element_type=F32).astype(BF16)
                place = ((zz >> 1) - meta[2]) & (NX - 1)
                mine = (zz & 1) == meta[3]

                @pl.when(mine)
                def _():
                    same[place, yy] = product

                @pl.when(jnp.logical_not(mine))
                def _():
                    other[place, yy] = product

            for_rows(low, high, step)

    shape = (NX, NY, BLK, TOK)
    return call(
        kernel,
        (meta, cols),
        [units_t, *chunks, *begun],
        (shaped(shape), shaped(shape)),
        {3 + len(chunks) + k: k for k in range(len(begun))},
    )


def pair_sums(meta, pairs):
    def kernel(meta, *refs):
        outs = refs[2 * len(pairs) :]
        for p in range(len(pairs)):
            for k in range(NX):
                total = refs[2 * p][k].astype(F32) + refs[2 * p + 1][k].astype(F32)
                outs[k][p] = total.astype(BF16)

    out = shaped((len(pairs), NY, BLK, TOK))
    return call(kernel, (meta,), [a for pair in pairs for a in pair], (out,) * NX)


def final_sums(meta, pieces):
    def kernel(meta, *refs):
        sources, outs = refs[: len(pieces)], refs[len(pieces) :]
        for p, out in enumerate(outs):
            for k in range(NY):
                total = sources[0][p, k].astype(F32)
                for ref in sources[1:]:
                    total = total + ref[p, k].astype(F32)
                out[:, k * BLK : (k + 1) * BLK] = total.astype(BF16).T

    out = shaped((TOK, FEAT))
    return call(kernel, (meta,), pieces, (out,) * pieces[0].shape[0])


def place_grads(meta, cols, pieces):
    def kernel(meta, cols, *refs):
        out = refs[-1]
        out[...] = jnp.zeros_like(out)
        base = (meta[0] * NY + meta[1]) * CAP
        for j in range(CAP):
            total = refs[0][j].astype(F32)
            for ref in refs[1:-1]:
                total = total + ref[j].astype(F32)
            col = cols[base + j]

            @pl.when(col >= 0)
            def _():
                out[:, lanes(jnp.maximum(col, 0))] = total.T

    shape = (BLK, FBT * BLK)
    return call(kernel, (meta, cols), pieces, shaped(shape, F32))


def column_tables(lists, counts):
    rows, cols = lists[:, :, 0], lists[:, :, 1]
    index = jnp.arange(lists.shape[1], dtype=jnp.int32)
    valid = index[None, :] < counts[:, None]
    rows = jnp.where(valid, rows, -1)
    same = (rows[:, :, None] == rows[:, None, :]) & (index[None, None, :] < index[None, :, None])
    rank = jnp.sum(same.astype(jnp.int32), axis=2)
    slot = jnp.where(valid, rows * CAP + rank, -1)
    chosen = slot[:, None, :] == index[None, :, None]
    return jnp.sum(jnp.where(chosen, cols[:, None, :] + 1, 0), axis=2) - 1


def body(tokens, cotangent, up_weight, down_weight, up_list, up_count, down_list, down_count):
    group, slice_id = lax.axis_index("fsdp"), lax.axis_index("tp")
    z, y = group // NY, group % NY
    meta = jnp.concatenate(
        [
            jnp.stack([z, y, slice_id // 2, slice_id % 2]),
            (z + jnp.array(ZD, jnp.int32)) & (NZ - 1),
            (y + jnp.array(YD, jnp.int32)) & (NY - 1),
        ]
    ).astype(jnp.int32)
    tables = column_tables(
        jnp.concatenate([up_list, down_list]), jnp.concatenate([up_count, down_count])
    )
    up_cols, down_cols = tables[0], tables[1]
    up_own, down_own, local = pick(meta, tables, up_weight, down_weight, tokens, cotangent)

    up_near = [shift_fsdp(up_own, 0, -d) for d in YD[1:]]
    da1, db1 = shift_fsdp(down_own, 1, 0), shift_fsdp(down_own, -1, 0)
    far = [shift_x(local, k) for k in (1, 2, 3)]
    u = join(meta, [up_own] + up_near)
    ua1, ub1 = shift_fsdp(u, 1, 0), shift_fsdp(u, -1, 0)
    da2, db2 = shift_fsdp(da1, 1, 0), shift_fsdp(db1, -1, 0)
    da3, db3 = shift_fsdp(da2, 1, 0), shift_fsdp(db2, -1, 0)
    da4 = shift_fsdp(da3, 1, 0)
    ua2, ub2 = shift_fsdp(ua1, 1, 0), shift_fsdp(ub1, -1, 0)
    dn = join(meta, [down_own, da1, db1, da2, db2, da3, db3, da4])
    dc1, dd1 = shift_fsdp(dn, 0, 1), shift_fsdp(dn, 0, -1)
    half = join(meta, [a[None] for a in (local, *far)])
    halves = (half, partner(half))
    ua3, ub3 = shift_fsdp(ua2, 1, 0), shift_fsdp(ub2, -1, 0)
    dc2 = shift_fsdp(lax.slice_in_dim(dc1, 0, 16), 0, 1)
    dd2 = shift_fsdp(lax.slice_in_dim(dd1, 16, 32), 0, -1)
    ua4 = shift_fsdp(lax.slice_in_dim(ua3, 0, 8), 1, 0)
    ub4 = shift_fsdp(lax.slice_in_dim(ub3, 8, 16), -1, 0)

    hidden = accumulate(
        meta, up_cols, 0, halves, (u, ua1, ub1),
        [("z", 0, 0, 0, 4), ("z", -1, 1, 0, 4), ("z", 1, 2, 0, 4)], None,
    )
    grad_active = accumulate(meta, down_cols, 1, halves, (dn,), [("y", 0, 0, 0, 8)], None)
    hidden = accumulate(
        meta, up_cols, 0, halves, (ua2, ub2),
        [("z", -2, 0, 0, 4), ("z", 2, 1, 0, 4)], hidden,
    )
    grad_active = accumulate(
        meta, down_cols, 1, halves, (dc1, dd1),
        [("y", -1, 0, 0, 8), ("y", 1, 1, 0, 8)], grad_active,
    )
    hidden = accumulate(
        meta, up_cols, 0, halves, (ua3, ub3),
        [("z", -3, 0, 0, 4), ("z", 3, 1, 0, 4)], hidden,
    )
    active_t, grad_hidden_t = finish(
        meta, up_cols, down_cols, halves, (ua4, ub4), (dc2, dd2), hidden, grad_active
    )

    def up_terms(offsets, received, sizes, segments):
        return terms(
            meta, up_cols, "z", 0, grad_hidden_t, halves, offsets, received, sizes, segments
        )

    def down_terms(offsets, received, sizes, segments):
        return terms(meta, down_cols, "y", 1, active_t, halves, offsets, received, sizes, segments)

    def both_ways_z(pair):
        return shift_fsdp(pair[0], 1, 0), shift_fsdp(pair[1], -1, 0)

    def both_ways_y(pair):
        return shift_fsdp(pair[0], 0, 1), shift_fsdp(pair[1], 0, -1)

    down = both_ways_y(down_terms((2,), (), (4, 4), [(0, 0, 4, 0, 0, ()), (0, 4, 8, 1, 4, ())]))
    up = both_ways_z(up_terms((4,), (), (2, 2), [(0, 0, 2, 0, 0, ()), (0, 2, 4, 1, 2, ())]))
    layer = project(meta, down_cols, "y", active_t, (dn, dc1), [(0, 0, 0, 8), (-1, 1, 0, 8)])
    layer = project(
        meta, down_cols, "y", active_t, (dd1, dc2, dd2),
        [(1, 0, 0, 8), (2, 1, 0, 4), (2, 2, 4, 8)], layer,
    )
    layer = (layer[0], partner(layer[1]))
    up = both_ways_z(up_terms(
        (3, -3), up, (4, 4),
        [(0, 0, 2, 0, 0, ((0, 0),)), (0, 2, 4, 0, 0, ()),
         (1, 0, 2, 1, 0, ()), (1, 2, 4, 1, 0, ((1, 2),))],
    ))
    down = both_ways_y(down_terms(
        (1, -1), down, (8, 8),
        [(0, 0, 4, 0, 0, ((0, 0),)), (0, 4, 8, 0, 0, ()),
         (1, 0, 4, 1, 0, ()), (1, 4, 8, 1, 0, ((1, 4),))],
    ))
    inputs = project(
        meta, up_cols, "z", grad_hidden_t, (u, ua1, ub1, ua2, ub2, ua3, ub3, ua4, ub4),
        [(ZD[i], i, 0, 4) for i in range(7)] + [(4, 7, 0, 2), (4, 8, 2, 4)],
    )
    inputs = (inputs[0], partner(inputs[1]))
    for k in (2, 1):
        up = both_ways_z(up_terms(
            (k, -k), up, (4, 4), [(0, 0, 4, 0, 0, ((0, 0),)), (1, 0, 4, 1, 0, ((1, 0),))]
        ))
    pair = pair_sums(meta, [layer, inputs])
    down_parts = down_terms(
        (0,), down, (1,) * NZ, [(0, i, i + 1, i, i, ((0, 0), (1, 0))) for i in range(NZ)]
    )
    up_parts = up_terms(
        (0,), up, (1,) * NY, [(0, i, i + 1, i, i, ((0, 0), (1, 0))) for i in range(NY)]
    )
    down_pieces = [down_parts[0]] + [shift_fsdp(down_parts[i], ZD[i], 0) for i in range(1, NZ)]
    up_pieces = [up_parts[0]] + [shift_fsdp(up_parts[i], 0, YD[i]) for i in range(1, NY)]
    mixed, grad_tokens = final_sums(meta, [pair[0]] + [shift_x(pair[k], k) for k in (1, 2, 3)])
    grad_down = place_grads(meta, down_cols, down_pieces)
    grad_up = place_grads(meta, up_cols, up_pieces)
    return (mixed, grad_tokens, grad_up, grad_down)


def solution(mesh):
    return jax.shard_map(
        body,
        mesh=mesh,
        in_specs=(
            P("fsdp", "tp"),
            P("fsdp", "tp"),
            P("fsdp", "tp"),
            P("fsdp", "tp"),
            P("tp", None, None),
            P("tp"),
            P("tp", None, None),
            P("tp"),
        ),
        out_specs=(P("fsdp", "tp"), P("fsdp", "tp"), P("fsdp", "tp"), P("fsdp", "tp")),
        check_vma=False,
    )
```

```python
import jax
import jax.numpy as jnp
from jax import lax
from jax.experimental import pallas as pl
from jax.experimental.pallas import tpu as pltpu
from jax.sharding import PartitionSpec as P


BLK = 128
CAP = 4
NZ, NY, NX = 8, 4, 4
FBT = 14
TOK = 256
FEAT = NY * BLK

SQRT_TWO_PI = 0.7978845608028654
CUBIC = 0.044715

ZD = (0, -1, 1, -2, 2, -3, 3, 4)
YD = (0, -1, 1, 2)

BF16 = jnp.bfloat16
F32 = jnp.float32

VMEM_LIMIT = 24 << 20


def shift_fsdp(value, dz, dy):
    pairs = []
    for z in range(NZ):
        for y in range(NY):
            pairs.append((z * NY + y, ((z + dz) % NZ) * NY + (y + dy) % NY))
    return lax.ppermute(value, "fsdp", pairs)


def shift_x(value, dx):
    return lax.ppermute(value, "tp", [(i, (i + 2 * dx) % 8) for i in range(8)])


def partner(value):
    return lax.ppermute(value, "tp", [(i, i ^ 1) for i in range(8)])


def z_at(meta, i):
    return meta[4 + i]


def y_at(meta, i):
    return meta[12 + i]


def lanes(index):
    return pl.ds(pl.multiple_of(index * BLK, BLK), BLK)


def read_features(halves, which, meta, zz, yy):
    place = (meta[2] - (zz >> 1)) & (NX - 1)
    mine = halves[0][place, which, :, lanes(yy)]
    theirs = halves[1][place, which, :, lanes(yy)]
    return jnp.where((zz & 1) == meta[3], mine, theirs)


def row_at(meta, kind, offset, i):
    if kind == "z":
        return z_at(meta, ZD.index(offset)), y_at(meta, i)
    return z_at(meta, i), y_at(meta, YD.index(offset))


def slot_cols(cols, zz, yy):
    base = (zz * NY + yy) * CAP
    return [jnp.maximum(cols[base + j], 0) for j in range(CAP)]


def for_rows(low, high, step, width=4):
    if high - low <= width:
        for i in range(low, high):
            step(i)
        return

    def turn(k, carry):
        for j in range(width):
            step(low + width * k + j)
        return carry

    lax.fori_loop(0, (high - low) // width, turn, 0)


def call(kernel, tables, operands, outs, aliases=None, scratch=(), space=pltpu.VMEM):
    vmem = pl.BlockSpec(memory_space=pltpu.VMEM)
    return pl.pallas_call(
        kernel,
        out_shape=outs,
        in_specs=[pl.BlockSpec(memory_space=pltpu.SMEM)] * len(tables)
        + [pl.BlockSpec(memory_space=space)] * len(operands),
        out_specs=(vmem,) * len(outs) if isinstance(outs, tuple) else vmem,
        scratch_shapes=scratch,
        input_output_aliases=aliases or {},
        compiler_params=pltpu.CompilerParams(vmem_limit_bytes=VMEM_LIMIT),
    )(*tables, *operands)


def shaped(shape, dtype=BF16):
    return jax.ShapeDtypeStruct(shape, dtype)


def pick(meta, both_cols, up_weight, down_weight, tokens, cotangent):
    def kernel(meta, cols, up_ref, down_ref, x_ref, dy_ref, up_out, down_out, both_out, sems):
        base = (meta[0] * NY + meta[1]) * CAP
        copies = [
            pltpu.make_async_copy(x_ref, both_out.at[0], sems.at[0]),
            pltpu.make_async_copy(dy_ref, both_out.at[1], sems.at[1]),
        ]
        blocks = []
        for part, (source, target) in enumerate(((up_ref, up_out), (down_ref, down_out))):
            for j in range(CAP):
                col = cols[part, base + j]
                blocks.append((col, target, j))
                copies.append(
                    pltpu.make_async_copy(
                        source.at[:, lanes(jnp.maximum(col, 0))],
                        target.at[j],
                        sems.at[2 + part * CAP + j],
                    )
                )
        for copy in copies:
            copy.start()
        for copy in copies:
            copy.wait()
        for col, target, j in blocks:

            @pl.when(col < 0)
            def _():
                target[j] = jnp.zeros((BLK, BLK), BF16)

    block = (CAP, BLK, BLK)
    both = (2, TOK, FEAT)
    return call(
        kernel,
        (meta, both_cols),
        [
            pltpu.with_memory_space_constraint(a, pltpu.HBM)
            for a in (up_weight, down_weight, tokens, cotangent)
        ],
        (shaped(block), shaped(block), shaped(both)),
        scratch=(pltpu.SemaphoreType.DMA((2 + 2 * CAP,)),),
        space=pltpu.HBM,
    )


def join(meta, pieces):
    sizes = [p.shape[0] for p in pieces]
    shape = (sum(sizes),) + pieces[0].shape[1:]

    def kernel(meta, *refs):
        at = 0
        for ref, size in zip(refs[:-1], sizes):
            refs[-1][at : at + size] = ref[...]
            at += size

    return call(kernel, (meta,), pieces, shaped(shape))


def add_products(meta, cols, which, segment, halves, chunk_refs, out):
    kind, offset, ci, low, high = segment

    def step(i):
        zz, yy = row_at(meta, kind, offset, i)
        left = read_features(halves, which, meta, zz, yy)
        base = (i - low) * CAP
        right = jnp.concatenate([chunk_refs[ci][base + j] for j in range(CAP)], axis=1)
        product = jnp.dot(left, right, preferred_element_type=F32)
        for j, col in enumerate(slot_cols(cols, zz, yy)):
            out[col] += product[:, j * BLK : (j + 1) * BLK]

    for_rows(low, high, step)


def accumulate(meta, cols, which, halves, chunks, segments, acc):
    def kernel(meta, cols, *refs):
        out = refs[-1]
        if acc is None:
            out[...] = jnp.zeros_like(out)
        for segment in segments:
            add_products(meta, cols, which, segment, refs[:2], refs[2:], out)

    operands = [*halves, *chunks]
    aliases = {}
    if acc is not None:
        operands.append(acc)
        aliases = {1 + len(operands): 0}
    return call(kernel, (meta, cols), operands, shaped((FBT, TOK, BLK), F32), aliases)


def finish(meta, up_cols, down_cols, halves, ups, downs, hidden, grad_active):
    def kernel(meta, up_cols, down_cols, own, other, *refs):
        up_refs, down_refs = refs[:2], refs[2:4]
        act_t, grad_t, h, g = refs[6:]
        for k in range(2):
            add_products(
                meta, up_cols, 0, ("z", 4, k, 2 * k, 2 * k + 2), (own, other), up_refs, h
            )
            add_products(
                meta, down_cols, 1, ("y", 2, k, 4 * k, 4 * k + 4), (own, other), down_refs, g
            )

        def step(c, carry):
            v = h[c]
            tangent = jnp.tanh(SQRT_TWO_PI * (v + CUBIC * v * v * v))
            slope = 0.5 * (1.0 + tangent) + 0.5 * v * (1.0 - tangent * tangent) * SQRT_TWO_PI * (
                1.0 + 3.0 * CUBIC * v * v
            )
            act_t[c] = (0.5 * v * (1.0 + tangent)).astype(BF16).T
            grad_t[c] = (g[c] * slope).astype(BF16).T
            return carry

        lax.fori_loop(0, FBT, step, 0)

    shape = (FBT, BLK, TOK)
    sums = shaped(hidden.shape, F32)
    return call(
        kernel,
        (meta, up_cols, down_cols),
        (*halves, *ups, *downs, hidden, grad_active),
        (shaped(shape), shaped(shape), sums, sums),
        {9: 2, 10: 3},
    )[:2]


def terms(meta, cols, kind, which, units_t, halves, offsets, received, sizes, segments):
    def kernel(meta, cols, own, other, units, *refs):
        got, outs = refs[: len(received)], refs[len(received) :]
        for oi, low, high, to, first, adds in segments:

            def step(i):
                zz, yy = row_at(meta, kind, offsets[oi], i)
                right = read_features((own, other), which, meta, zz, yy)
                left = jnp.concatenate([units[c] for c in slot_cols(cols, zz, yy)], axis=0)
                product = jnp.dot(left, right, preferred_element_type=F32)
                total = product.reshape(CAP, BLK, BLK)
                for gi, start in adds:
                    total = total + got[gi][pl.ds((i - start) * CAP, CAP)].astype(F32)
                outs[to][pl.ds((i - first) * CAP, CAP)] = total.astype(BF16)

            for_rows(low, high, step)

    return call(
        kernel,
        (meta, cols),
        [*halves, units_t, *received],
        tuple(shaped((size * CAP, BLK, BLK)) for size in sizes),
    )


def project(meta, cols, kind, units_t, chunks, segments, begun=()):
    def kernel(meta, cols, units, *refs):
        chunk_refs, (same, other) = refs[: len(chunks)], refs[-2:]
        for offset, ci, low, high in segments:

            def step(i):
                base = (i - low) * CAP
                left = jnp.concatenate([chunk_refs[ci][base + j] for j in range(CAP)], axis=1)
                zz, yy = row_at(meta, kind, offset, i)
                right = jnp.concatenate([units[c] for c in slot_cols(cols, zz, yy)], axis=0)
                product = jnp.dot(left, right, preferred_element_type=F32).astype(BF16)
                place = ((zz >> 1) - meta[2]) & (NX - 1)
                mine = (zz & 1) == meta[3]

                @pl.when(mine)
                def _():
                    same[place, yy] = product

                @pl.when(jnp.logical_not(mine))
                def _():
                    other[place, yy] = product

            for_rows(low, high, step, 2)

    shape = (NX, NY, BLK, TOK)
    return call(
        kernel,
        (meta, cols),
        [units_t, *chunks, *begun],
        (shaped(shape), shaped(shape)),
        {3 + len(chunks) + k: k for k in range(len(begun))},
    )


def pair_sums(meta, pairs):
    def kernel(meta, *refs):
        outs = refs[2 * len(pairs) :]
        for p in range(len(pairs)):
            for k in range(NX):
                total = refs[2 * p][k].astype(F32) + refs[2 * p + 1][k].astype(F32)
                outs[k][p] = total.astype(BF16)

    out = shaped((len(pairs), NY, BLK, TOK))
    return call(kernel, (meta,), [a for pair in pairs for a in pair], (out,) * NX)


def final_sums(meta, pieces):
    def kernel(meta, *refs):
        sources, outs = refs[: len(pieces)], refs[len(pieces) :]
        for p, out in enumerate(outs):
            for k in range(NY):
                total = sources[0][p, k].astype(F32)
                for ref in sources[1:]:
                    total = total + ref[p, k].astype(F32)
                out[:, k * BLK : (k + 1) * BLK] = total.astype(BF16).T

    out = shaped((TOK, FEAT))
    return call(kernel, (meta,), pieces, (out,) * pieces[0].shape[0])


def place_grads(meta, cols, pieces):
    def kernel(meta, cols, *refs):
        out = refs[-1]
        out[...] = jnp.zeros_like(out)
        base = (meta[0] * NY + meta[1]) * CAP
        for j in range(CAP):
            total = refs[0][j].astype(F32)
            for ref in refs[1:-1]:
                total = total + ref[j].astype(F32)
            col = cols[base + j]

            @pl.when(col >= 0)
            def _():
                out[:, lanes(jnp.maximum(col, 0))] = total.T

    shape = (BLK, FBT * BLK)
    return call(kernel, (meta, cols), pieces, shaped(shape, F32))


def column_tables(lists, counts):
    rows, cols = lists[:, :, 0], lists[:, :, 1]
    index = jnp.arange(lists.shape[1], dtype=jnp.int32)
    valid = index[None, :] < counts[:, None]
    rows = jnp.where(valid, rows, -1)
    same = (rows[:, :, None] == rows[:, None, :]) & (index[None, None, :] < index[None, :, None])
    rank = jnp.sum(same.astype(jnp.int32), axis=2)
    slot = jnp.where(valid, rows * CAP + rank, -1)
    chosen = slot[:, None, :] == index[None, :, None]
    return jnp.sum(jnp.where(chosen, cols[:, None, :] + 1, 0), axis=2) - 1


def body(tokens, cotangent, up_weight, down_weight, up_list, up_count, down_list, down_count):
    group, slice_id = lax.axis_index("fsdp"), lax.axis_index("tp")
    z, y = group // NY, group % NY
    meta = jnp.concatenate(
        [
            jnp.stack([z, y, slice_id // 2, slice_id % 2]),
            (z + jnp.array(ZD, jnp.int32)) & (NZ - 1),
            (y + jnp.array(YD, jnp.int32)) & (NY - 1),
        ]
    ).astype(jnp.int32)
    tables = column_tables(
        jnp.concatenate([up_list, down_list]), jnp.concatenate([up_count, down_count])
    )
    up_cols, down_cols = tables[0], tables[1]
    up_own, down_own, local = pick(meta, tables, up_weight, down_weight, tokens, cotangent)

    up_near = [shift_fsdp(up_own, 0, -d) for d in YD[1:]]
    da1, db1 = shift_fsdp(down_own, 1, 0), shift_fsdp(down_own, -1, 0)
    far = [shift_x(local, k) for k in (1, 2, 3)]
    u = join(meta, [up_own] + up_near)
    ua1, ub1 = shift_fsdp(u, 1, 0), shift_fsdp(u, -1, 0)
    da2, db2 = shift_fsdp(da1, 1, 0), shift_fsdp(db1, -1, 0)
    da3, db3 = shift_fsdp(da2, 1, 0), shift_fsdp(db2, -1, 0)
    da4 = shift_fsdp(da3, 1, 0)
    ua2, ub2 = shift_fsdp(ua1, 1, 0), shift_fsdp(ub1, -1, 0)
    dn = join(meta, [down_own, da1, db1, da2, db2, da3, db3, da4])
    dc1, dd1 = shift_fsdp(dn, 0, 1), shift_fsdp(dn, 0, -1)
    half = join(meta, [a[None] for a in (local, *far)])
    halves = (half, partner(half))
    ua3, ub3 = shift_fsdp(ua2, 1, 0), shift_fsdp(ub2, -1, 0)
    dc2 = shift_fsdp(lax.slice_in_dim(dc1, 0, 16), 0, 1)
    dd2 = shift_fsdp(lax.slice_in_dim(dd1, 16, 32), 0, -1)
    ua4 = shift_fsdp(lax.slice_in_dim(ua3, 0, 8), 1, 0)
    ub4 = shift_fsdp(lax.slice_in_dim(ub3, 8, 16), -1, 0)

    hidden = accumulate(
        meta, up_cols, 0, halves, (u, ua1, ub1),
        [("z", 0, 0, 0, 4), ("z", -1, 1, 0, 4), ("z", 1, 2, 0, 4)], None,
    )
    grad_active = accumulate(meta, down_cols, 1, halves, (dn,), [("y", 0, 0, 0, 8)], None)
    hidden = accumulate(
        meta, up_cols, 0, halves, (ua2, ub2),
        [("z", -2, 0, 0, 4), ("z", 2, 1, 0, 4)], hidden,
    )
    grad_active = accumulate(
        meta, down_cols, 1, halves, (dc1, dd1),
        [("y", -1, 0, 0, 8), ("y", 1, 1, 0, 8)], grad_active,
    )
    hidden = accumulate(
        meta, up_cols, 0, halves, (ua3, ub3),
        [("z", -3, 0, 0, 4), ("z", 3, 1, 0, 4)], hidden,
    )
    active_t, grad_hidden_t = finish(
        meta, up_cols, down_cols, halves, (ua4, ub4), (dc2, dd2), hidden, grad_active
    )

    def up_terms(offsets, received, sizes, segments):
        return terms(
            meta, up_cols, "z", 0, grad_hidden_t, halves, offsets, received, sizes, segments
        )

    def down_terms(offsets, received, sizes, segments):
        return terms(meta, down_cols, "y", 1, active_t, halves, offsets, received, sizes, segments)

    def both_ways_z(pair):
        return shift_fsdp(pair[0], 1, 0), shift_fsdp(pair[1], -1, 0)

    def both_ways_y(pair):
        return shift_fsdp(pair[0], 0, 1), shift_fsdp(pair[1], 0, -1)

    down = both_ways_y(down_terms((2,), (), (4, 4), [(0, 0, 4, 0, 0, ()), (0, 4, 8, 1, 4, ())]))
    up = both_ways_z(up_terms((4,), (), (2, 2), [(0, 0, 2, 0, 0, ()), (0, 2, 4, 1, 2, ())]))
    layer = project(meta, down_cols, "y", active_t, (dn, dc1), [(0, 0, 0, 8), (-1, 1, 0, 8)])
    layer = project(
        meta, down_cols, "y", active_t, (dd1, dc2, dd2),
        [(1, 0, 0, 8), (2, 1, 0, 4), (2, 2, 4, 8)], layer,
    )
    layer = (layer[0], partner(layer[1]))
    up = both_ways_z(up_terms(
        (3, -3), up, (4, 4),
        [(0, 0, 2, 0, 0, ((0, 0),)), (0, 2, 4, 0, 0, ()),
         (1, 0, 2, 1, 0, ()), (1, 2, 4, 1, 0, ((1, 2),))],
    ))
    down = both_ways_y(down_terms(
        (1, -1), down, (8, 8),
        [(0, 0, 4, 0, 0, ((0, 0),)), (0, 4, 8, 0, 0, ()),
         (1, 0, 4, 1, 0, ()), (1, 4, 8, 1, 0, ((1, 4),))],
    ))
    inputs = project(
        meta, up_cols, "z", grad_hidden_t, (u, ua1, ub1, ua2, ub2, ua3, ub3, ua4, ub4),
        [(ZD[i], i, 0, 4) for i in range(7)] + [(4, 7, 0, 2), (4, 8, 2, 4)],
    )
    inputs = (inputs[0], partner(inputs[1]))
    for k in (2, 1):
        up = both_ways_z(up_terms(
            (k, -k), up, (4, 4), [(0, 0, 4, 0, 0, ((0, 0),)), (1, 0, 4, 1, 0, ((1, 0),))]
        ))
    pair = pair_sums(meta, [layer, inputs])
    down_parts = down_terms(
        (0,), down, (1,) * NZ, [(0, i, i + 1, i, i, ((0, 0), (1, 0))) for i in range(NZ)]
    )
    up_parts = up_terms(
        (0,), up, (1,) * NY, [(0, i, i + 1, i, i, ((0, 0), (1, 0))) for i in range(NY)]
    )
    down_pieces = [down_parts[0]] + [shift_fsdp(down_parts[i], ZD[i], 0) for i in range(1, NZ)]
    up_pieces = [up_parts[0]] + [shift_fsdp(up_parts[i], 0, YD[i]) for i in range(1, NY)]
    mixed, grad_tokens = final_sums(meta, [pair[0]] + [shift_x(pair[k], k) for k in (1, 2, 3)])
    grad_down = place_grads(meta, down_cols, down_pieces)
    grad_up = place_grads(meta, up_cols, up_pieces)
    return (mixed, grad_tokens, grad_up, grad_down)


def solution(mesh):
    return jax.shard_map(
        body,
        mesh=mesh,
        in_specs=(
            P("fsdp", "tp"),
            P("fsdp", "tp"),
            P("fsdp", "tp"),
            P("fsdp", "tp"),
            P("tp", None, None),
            P("tp"),
            P("tp", None, None),
            P("tp"),
        ),
        out_specs=(P("fsdp", "tp"), P("fsdp", "tp"), P("fsdp", "tp"), P("fsdp", "tp")),
        check_vma=False,
    )
```
